512 devices in a mesh: cells: 64 (over y_hi, z, x), tensor: 8 (over y_lo, core).
Axes of the slice: x: 4, y: 8 (y_hi: 2, y_lo: 4; y = y_hi * 4 + y_lo), z: 8, core: 2. Of those that a mesh axis runs over, the one named last changes fastest.
Arguments:
- features: bfloat16 [65536, 512], P(('cells', 'tensor')), may hold values from -48 to 48
- cotangent: bfloat16 [65536, 512], P(('cells', 'tensor')), may hold values from -6 to 6
- first_gain: float32 [512], replicated, may hold values from 0.5 to 1.5
- project_weight: bfloat16 [3, 512, 512], replicated, may hold values from -1 to 1
- output_weight: bfloat16 [512, 512], replicated, may hold values from -0.25 to 0.25
- neighbours: int32 [65536, 64], P(('cells', 'tensor')), may hold values from 0 to 191, as said below
- neighbour_live: int32 [65536, 64], P(('cells', 'tensor')), may hold values from 0 to 1, as said below
- send_rows: int32 [2048, 16], P(('cells', 'tensor')), may hold values from 0 to 127
Outputs:
- layer_output: bfloat16 [65536, 512], P(('cells', 'tensor'))
- grad_features: float32 [65536, 512], P(('cells', 'tensor'))
- grad_project: float32 [786432], P(('cells', 'tensor'))
- grad_output: float32 [262144], P(('cells', 'tensor'))
The draws below stay inside these ranges and needn't reach their ends.
Inputs may be any that keep to these rules, and one draw needn't show every extreme that they name: `neighbours`: entry 0 of each row is the cell's own row within its block. `neighbour_live`: entry 0 of each row is 1, and the ones of a row come first.
All inputs are finite; a program needn't handle non-finite values.
Results may differ from the reference program's by a relative error of at most 0.0055.
The reference program's roundings to bfloat16 on the way (of `first`, `rounded`, `mixed`, `grad_mixed` and `grad_qkv`) count: a program that leaves them out, or rounds other values in their place, can miss the bound.
Values may be sent and summed in bfloat16 or wider, within the bound.
No kernel may reach another device: no remote copies, remote signals or barrier semaphores. Data moves between devices by JAX's collectives and lax.ppermute only.
A program may use at most 64 MiB of HBM per device.

```python
import math
import jax
import jax.numpy as jnp
from jax import lax

D = 512
HEADS = 8
HEAD_DIM = 64
NEIGHBOURS = 64
C_DEV = 128
CAP = 16
CELLS = 65536
N_CELLS = 64
N_TENSOR = 8


def draw_features(key, part):
    cell_count = C_DEV * N_CELLS * N_TENSOR
    row_key, column_key, noise_key = jax.random.split(jax.random.fold_in(key, 101), 3)
    row_scale = jnp.exp(jax.random.uniform(row_key, (cell_count, 1), jnp.float32, math.log(0.5), math.log(4.0)))
    column_scale = jnp.exp(jax.random.uniform(column_key, (1, D), jnp.float32, math.log(0.5), math.log(4.0)))
    result = jnp.clip(jax.random.normal(noise_key, (cell_count, D), jnp.float32), -3.0, 3.0) * row_scale * column_scale
    return jnp.clip(result, -48.0, 48.0).astype(jnp.bfloat16)


def draw_project_weight(key, part):
    head_span = HEADS * HEAD_DIM
    base_key = jax.random.fold_in(jax.random.fold_in(key, 202), 0)
    result = jnp.clip(jax.random.normal(base_key, (3, D, head_span), jnp.float32), -3.0, 3.0) / math.sqrt(D)
    return result.astype(jnp.bfloat16)


def draw_neighbours(key, part):
    block_total = N_CELLS * N_TENSOR
    cell_count = C_DEV * block_total
    keys_list = jax.random.split(jax.random.fold_in(key, 303), 6)
    reach_cells = max(C_DEV // 8, 1)
    local_row = jnp.arange(cell_count, dtype=jnp.int32) % C_DEV
    shifted = jnp.clip(local_row[:, None] + jax.random.randint(keys_list[0], (cell_count, NEIGHBOURS), -reach_cells, reach_cells + 1), 0, C_DEV - 1)
    live_count = jax.random.randint(keys_list[1], (block_total, 4), CAP // 2, CAP + 1)
    direction = jax.random.randint(keys_list[2], (cell_count, NEIGHBOURS), 0, 4)
    group_index = (jnp.arange(cell_count, dtype=jnp.int32) // C_DEV)[:, None]
    slot_limit = live_count[group_index, direction]
    slot_index = jax.random.randint(keys_list[3], (cell_count, NEIGHBOURS), 0, slot_limit)
    remote = C_DEV + direction * CAP + slot_index
    is_remote = jax.random.randint(keys_list[4], (cell_count, NEIGHBOURS), 0, 4) == 0
    result = jnp.where(is_remote, remote, shifted)
    result = result.at[:, 0].set(local_row)
    forced = jax.random.randint(keys_list[5], (), 0, cell_count)
    result = result.at[forced, 1].set(C_DEV + 4 * CAP - 1)
    return result.astype(jnp.int32)


def draw_neighbour_live(key, part):
    cell_count = C_DEV * N_CELLS * N_TENSOR
    live_total = jax.random.randint(jax.random.fold_in(key, 404), (cell_count, 1), NEIGHBOURS * 3 // 4, NEIGHBOURS + 1)
    return (jnp.arange(NEIGHBOURS, dtype=jnp.int32)[None, :] < live_total).astype(jnp.int32)


def draw_send_rows(key, part):
    list_count = 4 * N_CELLS * N_TENSOR
    keys_list = jax.random.split(jax.random.fold_in(key, 505), 5)
    result = jax.random.randint(keys_list[0], (list_count, CAP), 0, C_DEV)
    first_at = jax.random.randint(keys_list[1], (), 0, list_count)
    first_slot = jax.random.randint(keys_list[2], (), 0, CAP)
    second_at = jax.random.randint(keys_list[3], (), 0, list_count)
    second_slot = jax.random.randint(keys_list[4], (), 0, CAP)
    result = result.at[first_at, first_slot].set(0)
    result = result.at[second_at, second_slot].set(C_DEV - 1)
    return result.astype(jnp.int32)


def block_scale(rng, dims, shards, low, largest):
    loudness = 1.0
    for position, parts in shards:
        heights = jax.random.uniform(jax.random.fold_in(jax.random.fold_in(rng, 6), position), (parts,), jnp.float32, low / len(shards), largest / len(shards))
        loudness = loudness * jnp.repeat(jnp.exp(heights), dims[position] // parts).reshape((-1,) + (1,) * (len(dims) - 1 - position))
    return loudness


def scatter_about(stream_key, shape, width, bound, cuts=(), held_as=jnp.bfloat16):
    values = width * jax.random.normal(stream_key, shape, jnp.float32)
    if cuts:
        values = values * block_scale(stream_key, shape, cuts, -0.22, 0.18)
    return jnp.clip(values, -bound, bound).astype(held_as)


def setup_inputs(seed: int = 0) -> dict:
    seeds = jax.random.split(jax.random.key(seed), 9)
    return {
        "features": draw_features(jax.random.fold_in(seeds[8], 71), 0),
        "cotangent": scatter_about(seeds[1], (CELLS, D), 1.0, 6.0, ((0, 512),)),
        "first_gain": jnp.clip(1.0 + 0.1 * jax.random.normal(seeds[2], (D,), jnp.float32), 0.5, 1.5),
        "project_weight": draw_project_weight(jax.random.fold_in(seeds[8], 71), 0),
        "output_weight": scatter_about(seeds[4], (HEADS * HEAD_DIM, D), (HEADS * HEAD_DIM) ** -0.5, 0.25),
        "neighbours": draw_neighbours(jax.random.fold_in(seeds[8], 71), 0),
        "neighbour_live": draw_neighbour_live(jax.random.fold_in(seeds[8], 71), 0),
        "send_rows": draw_send_rows(jax.random.fold_in(seeds[8], 71), 0),
    }


EPSILON = 1e-06

def norm_rows(inputs, gain):
    values = inputs.astype(jnp.float32)
    factor = lax.rsqrt(lax.optimization_barrier(jnp.mean(values * values, axis=-1, keepdims=True)) + EPSILON)
    return (values * factor * gain).astype(jnp.bfloat16)

def norm_back(inputs, gain, upstream):
    values = inputs.astype(jnp.float32)
    factor = lax.rsqrt(lax.optimization_barrier(jnp.mean(values * values, axis=-1, keepdims=True)) + EPSILON)
    weighted = upstream * gain
    return factor * weighted - values * factor ** 3 * lax.optimization_barrier(jnp.mean(values * weighted, axis=-1, keepdims=True))

def sources(neighbours, send_rows):
    cell_count = neighbours.shape[0]
    block = (jnp.arange(cell_count, dtype=jnp.int32) // C_DEV)[:, None]
    along = block // N_TENSOR
    across = block % N_TENSOR
    extra = neighbours - C_DEV
    direction = jnp.clip(extra // CAP, 0, 3).astype(jnp.int32)
    slot_index = jnp.where(extra >= 0, extra % CAP, 0).astype(jnp.int32)
    across_step = jnp.array([-1, 1, 0, 0], dtype=jnp.int32)[direction]
    along_step = jnp.array([0, 0, -1, 1], dtype=jnp.int32)[direction]
    peer = (jnp.mod(along + along_step, N_CELLS) * N_TENSOR + jnp.mod(across + across_step, N_TENSOR)).astype(jnp.int32)
    remote = peer * C_DEV + send_rows[peer * 4 + direction, slot_index]
    return jnp.where(extra >= 0, remote, block * C_DEV + neighbours).astype(jnp.int32)

def softmax_weights(query_heads, key_rows, live_rows):
    scores = jnp.einsum('bhe,bkhe->bhk', query_heads.astype(jnp.float32), key_rows.astype(jnp.float32), precision=lax.Precision.HIGHEST)
    scores = scores * query_heads.shape[-1] ** (-0.5)
    is_live = (live_rows > 0)[:, None, :]
    scores = jnp.where(is_live, scores, -1e+30)
    row_max = lax.optimization_barrier(jnp.max(scores, axis=-1, keepdims=True))
    weights = jnp.where(is_live, jnp.exp(scores - row_max), 0.0)
    probabilities = weights / lax.optimization_barrier(jnp.sum(weights, axis=-1, keepdims=True))
    return (probabilities, probabilities.astype(jnp.bfloat16))

def reference(features, cotangent, first_gain, project_weight, output_weight, neighbours, neighbour_live, send_rows):
    cell_count = features.shape[0]
    block_count = cell_count // C_DEV
    head_span = HEADS * HEAD_DIM
    grad_scale = float(cell_count) ** (-0.5)
    highest = lax.Precision.HIGHEST
    first = norm_rows(features, first_gain)
    queries, keys, values = [jnp.dot(first, project_weight[part_index], preferred_element_type=jnp.float32).astype(jnp.bfloat16) for part_index in range(3)]
    source = sources(neighbours, send_rows)
    key_heads = keys.reshape(cell_count, HEADS, HEAD_DIM)
    value_heads = values.reshape(cell_count, HEADS, HEAD_DIM)
    query_groups = queries.reshape(block_count, C_DEV, HEADS, HEAD_DIM)
    source_groups = source.reshape(block_count, C_DEV, NEIGHBOURS)
    live_groups = neighbour_live.reshape(block_count, C_DEV, NEIGHBOURS)

    def forward_group(inputs_group):
        query_heads, source_rows, live_rows = inputs_group
        probabilities, rounded = softmax_weights(query_heads, key_heads[source_rows], live_rows)
        mixed_heads = jnp.einsum('bhk,bkhe->bhe', rounded.astype(jnp.float32), value_heads[source_rows].astype(jnp.float32), precision=highest)
        return mixed_heads.astype(jnp.bfloat16)
    mixed = lax.map(forward_group, (query_groups, source_groups, live_groups)).reshape(cell_count, head_span)
    layer_output = (features.astype(jnp.float32) + jnp.dot(mixed, output_weight, preferred_element_type=jnp.float32)).astype(jnp.bfloat16)
    grad_mixed = jnp.dot(cotangent, output_weight.T, preferred_element_type=jnp.float32).astype(jnp.bfloat16)
    grad_output = jnp.dot(cotangent.T, mixed, preferred_element_type=jnp.float32)
    factor = HEAD_DIM ** (-0.5)

    def back_group(carry, inputs_group):
        key_sum, value_sum = carry
        query_heads, source_rows, live_rows, upstream = inputs_group
        key_rows = key_heads[source_rows].astype(jnp.float32)
        value_rows = value_heads[source_rows].astype(jnp.float32)
        probabilities, rounded = softmax_weights(query_heads, key_rows, live_rows)
        upstream_heads = upstream.astype(jnp.float32)
        grad_probs = jnp.einsum('bhe,bkhe->bhk', upstream_heads, value_rows, precision=highest)
        grad_scores = probabilities * (grad_probs - lax.optimization_barrier(jnp.sum(probabilities * grad_probs, axis=-1, keepdims=True)))
        grad_query = jnp.einsum('bhk,bkhe->bhe', grad_scores, key_rows, precision=highest) * factor
        grad_keys = jnp.einsum('bhk,bhe->bkhe', grad_scores, query_heads.astype(jnp.float32), precision=highest) * factor
        grad_values = jnp.einsum('bhk,bhe->bkhe', rounded.astype(jnp.float32), upstream_heads, precision=highest)
        flat_index = source_rows.reshape(-1)
        key_sum = key_sum.at[flat_index].add(grad_keys.reshape(-1, HEADS, HEAD_DIM))
        value_sum = value_sum.at[flat_index].add(grad_values.reshape(-1, HEADS, HEAD_DIM))
        return ((key_sum, value_sum), grad_query)
    start_grads = (jnp.zeros((cell_count, HEADS, HEAD_DIM), jnp.float32), jnp.zeros((cell_count, HEADS, HEAD_DIM), jnp.float32))
    (key_sum, value_sum), grad_queries = lax.scan(back_group, start_grads, (query_groups, source_groups, live_groups, grad_mixed.reshape(block_count, C_DEV, HEADS, HEAD_DIM)))
    grad_qkv = jnp.stack([grad_queries.reshape(cell_count, head_span), key_sum.reshape(cell_count, head_span), value_sum.reshape(cell_count, head_span)]).astype(jnp.bfloat16)
    grad_project = jnp.stack([jnp.dot(first.T, grad_qkv[part_index], preferred_element_type=jnp.float32) for part_index in range(3)])
    grad_first = jnp.zeros((cell_count, D), jnp.float32)
    for part_index in range(3):
        grad_first = grad_first + jnp.dot(grad_qkv[part_index], project_weight[part_index].T, preferred_element_type=jnp.float32)
    grad_features = cotangent.astype(jnp.float32) + norm_back(features, first_gain, grad_first)
    return (layer_output, grad_features, (grad_project * grad_scale).reshape(-1), (grad_output * grad_scale).reshape(-1))
```

```python
import math

import jax
import jax.numpy as jnp
import numpy as np
from jax import lax
from jax.experimental import pallas as pl
from jax.experimental.pallas import tpu as pltpu
from jax.sharding import Mesh
from jax.sharding import PartitionSpec as P

HEADS = 8
HEAD_DIM = 64
EPSILON = 1e-06
F32 = jnp.float32
BF16 = jnp.bfloat16
AXES = ("yh", "z", "x", "yl", "core")
CELLS = ("yh", "z", "x")
TENSOR = ("yl", "core")
FAR = ("yh", "z", "yl")


def dot(a, b, dims=((1,), (0,))):
    return lax.dot_general(a, b, (dims, ((), ())), preferred_element_type=F32)


def split(values):
    high = values.astype(BF16)
    return high, (values - high.astype(F32)).astype(BF16)


def call(kernel, out_shapes, args, us, scalars=0, scratch=()):
    specs = [pl.BlockSpec(memory_space=pltpu.SMEM)] * scalars
    specs += [pl.BlockSpec(memory_space=pltpu.VMEM)] * (len(args) - scalars)
    return pl.pallas_call(
        kernel,
        out_shape=out_shapes,
        in_specs=specs,
        out_specs=jax.tree.map(lambda _: pl.BlockSpec(memory_space=pltpu.VMEM), out_shapes),
        scratch_shapes=list(scratch),
        cost_estimate=pl.CostEstimate(
            flops=int(us * 4e8), bytes_accessed=int(us * 1e6), transcendentals=0
        ),
    )(*args)


def shape(*dims, dtype=BF16):
    return jax.ShapeDtypeStruct(dims, dtype)


def norm_factor(values):
    return lax.rsqrt(jnp.mean(values * values, axis=-1, keepdims=True) + EPSILON)


def keys_kernel(features, gain, weight, send_rows, first, key_values, *bands):
    values = features[...].astype(F32)
    normed = (values * norm_factor(values) * gain[...]).astype(BF16)
    first[...] = normed
    width = weight.shape[2]
    for part in range(2):
        key_values[:, part * width : (part + 1) * width] = dot(normed, weight[1 + part]).astype(
            BF16
        )
    table = key_values[...]
    rows, cap = features.shape[0], send_rows.shape[1]
    row_ids = lax.broadcasted_iota(jnp.int32, (rows, cap), 0)
    for direction in range(4):
        chosen = (row_ids == send_rows[direction : direction + 1, :]).astype(F32).astype(BF16)
        bands[direction][...] = dot(chosen, table, ((0,), (0,))).astype(BF16)


def queries_kernel(
    first, weight, output_weight, cotangent, neighbours, live, queries, grad_mixed, counts
):
    queries[...] = dot(first[...], weight[0]).astype(BF16)
    grad_mixed[...] = dot(cotangent[...], output_weight[...], ((1,), (1,))).astype(BF16)
    slots = jnp.where(live[...] > 0, neighbours[...], -1)
    rows = slots.shape[0]
    columns = lax.broadcasted_iota(jnp.int32, (rows, counts.shape[1]), 1)
    total = jnp.zeros(columns.shape, F32)
    for slot in range(slots.shape[1]):
        total = total + jnp.where(slots[:, slot : slot + 1] == columns, 1.0, 0.0)
    counts[...] = total


def attention_kernel(
    queries, key_values, band0, band1, band2, band3, grad_mixed, counts, first, cotangent,
    sent, own, back0, back1, back2, back3, table, grads,
):
    rows, width = queries.shape
    cap = band0.shape[0]
    table[:rows, :] = key_values[...]
    for direction, band in enumerate((band0, band1, band2, band3)):
        start = rows + direction * cap
        table[start : start + cap, :] = band[...]
    factor = HEAD_DIM**-0.5
    count = counts[...]
    is_live = count > 0
    wide = 2 * HEAD_DIM
    side = lax.broadcasted_iota(jnp.int32, (1, wide), 1) // HEAD_DIM
    for pair in range(HEADS // 2):
        lanes = slice(pair * wide, (pair + 1) * wide)
        value_lanes = slice(width + pair * wide, width + (pair + 1) * wide)
        query, upstream = queries[:, lanes], grad_mixed[:, lanes]
        key, value = table[:, lanes], table[:, value_lanes]
        zero = jnp.zeros((), BF16)
        mixed, grad_query, grad_key, grad_value = [], [], None, None
        for half in range(2):
            mine = side == half
            query_half = jnp.where(mine, query, zero)
            upstream_half = jnp.where(mine, upstream, zero)
            scores = dot(query_half, key, ((1,), (1,))) * factor
            grad_probs = dot(upstream_half, value, ((1,), (1,)))
            scores = jnp.where(is_live, scores, -1e30)
            row_max = jnp.max(scores, axis=-1, keepdims=True)
            powers = jnp.where(is_live, jnp.exp(scores - row_max), 0.0)
            probabilities = powers / jnp.sum(count * powers, axis=-1, keepdims=True)
            weights = split(count * probabilities.astype(BF16).astype(F32))
            spread = count * probabilities
            grad_scores = spread * (
                grad_probs - jnp.sum(spread * grad_probs, axis=-1, keepdims=True)
            )
            grad_scores = split(grad_scores * factor)
            mixed.append(dot(weights[0], value) + dot(weights[1], value))
            grad_query.append(dot(grad_scores[0], key) + dot(grad_scores[1], key))
            grad_k = sum(dot(g, query_half, ((0,), (0,))) for g in grad_scores)
            grad_v = sum(dot(w, upstream_half, ((0,), (0,))) for w in weights)
            grad_key = grad_k if half == 0 else grad_key + grad_k
            grad_value = grad_v if half == 0 else grad_value + grad_v
        at = 2 * width + pair * wide
        sent[:, at : at + wide] = jnp.where(side == 0, mixed[0], mixed[1]).astype(BF16)
        at = 3 * width + pair * wide
        sent[:, at : at + wide] = jnp.where(side == 0, grad_query[0], grad_query[1]).astype(BF16)
        grads[:, lanes] = grad_key
        grads[:, value_lanes] = grad_value
    own[...] = grads[:rows, :]
    for direction, back in enumerate((back0, back1, back2, back3)):
        start = rows + direction * cap
        back[...] = grads[start : start + cap, :].astype(BF16)
    sent[:, :width] = first[...]
    sent[:, width : 2 * width] = cotangent[...]


def layer_kernel(features, sent, output_weight, layer_output):
    width = features.shape[1]
    mixed = sent[:, 2 * width : 3 * width]
    layer_output[...] = (features[...].astype(F32) + dot(mixed, output_weight[...])).astype(BF16)


def chosen_kernel(core, sent, partner, feature_of, cell_of, per_core, left, grad_output):
    rows, width = sent.shape[0], grad_output.shape[1]
    offset = core[0, 0]
    columns = lax.broadcasted_iota(jnp.int32, (feature_of.shape[0], width), 1)
    target = feature_of[...] + offset * per_core[0, 0]
    feature = jnp.bitwise_and(target, width - 1)
    chosen = (feature == columns).astype(F32).astype(BF16)
    part = jnp.right_shift(target, width.bit_length() - 1)
    for index, source in enumerate((sent, partner)):
        picked = dot(chosen, source[:, :width], ((1,), (1,)))
        for piece in range(3):
            at = (2 * piece + index) * rows
            left[:, at : at + rows] = jnp.where(part == piece, picked, 0.0).astype(BF16)
    columns = lax.broadcasted_iota(jnp.int32, (cell_of.shape[0], width), 1)
    chosen = (cell_of[...] + offset * per_core[0, 1] == columns).astype(F32).astype(BF16)
    total = None
    for source in (sent, partner):
        picked = dot(chosen, source[:, width : 2 * width], ((1,), (1,))).astype(BF16)
        product = dot(picked, source[:, 2 * width : 3 * width])
        total = product if total is None else total + product
    grad_output[...] = total


def merge_kernel(own, back0, back1, back2, back3, send_rows, grad_keys_values):
    rows, cap = own.shape[0], send_rows.shape[1]
    row_ids = lax.broadcasted_iota(jnp.int32, (rows, cap), 0)
    total = own[...]
    for direction, back in enumerate((back0, back1, back2, back3)):
        chosen = (row_ids == send_rows[direction : direction + 1, :]).astype(F32).astype(BF16)
        total = total + dot(chosen, back[...])
    grad_keys_values[...] = total.astype(BF16)


def project_kernel(left, sent, partner, own_grads, partner_grads, grad_project, right):
    rows, width = sent.shape[0], grad_project.shape[1]
    for index, (early, late) in enumerate(((sent, own_grads), (partner, partner_grads))):
        pieces = (
            early[:, 3 * width : 4 * width],
            late[:, :width],
            late[:, width : 2 * width],
        )
        for piece in range(3):
            at = (2 * piece + index) * rows
            right[at : at + rows, :] = pieces[piece]
    grad_project[...] = dot(left[...], right[...])


def features_kernel(features, cotangent, gain, sent, late, weight, grad_features):
    width = features.shape[1]
    grad_first = dot(sent[:, 3 * width : 4 * width], weight[0], ((1,), (1,)))
    for part in range(2):
        grad_first = grad_first + dot(
            late[:, part * width : (part + 1) * width], weight[1 + part], ((1,), (1,))
        )
    values = features[...].astype(F32)
    factor = norm_factor(values)
    weighted = grad_first * gain[...]
    mean = jnp.mean(values * weighted, axis=-1, keepdims=True)
    grad_features[...] = cotangent[...].astype(F32) + (
        factor * weighted - values * factor**3 * mean
    )


def near_kernel(project, output, summed):
    far = summed.shape[0]
    for source, first_row in ((project, 0), (output, summed.shape[1] - output.shape[1] // far)):
        total = source[0]
        for index in range(1, source.shape[0]):
            total = total + source[index]
        for row in range(source.shape[1] // far):
            summed[:, first_row + row, :] = total[row * far : (row + 1) * far, :]


def far_kernel(scale, parts, grad_project, grad_output):
    total = jnp.sum(parts[...], axis=0) * scale
    lanes = grad_project.shape[1]
    per_row = total.shape[1] // lanes
    project_rows = grad_project.shape[0] // per_row
    for row in range(total.shape[0]):
        for piece in range(per_row):
            values = total[row : row + 1, piece * lanes : (piece + 1) * lanes]
            if row < project_rows:
                grad_project[row * per_row + piece : row * per_row + piece + 1, :] = values
            else:
                at = (row - project_rows) * per_row + piece
                grad_output[at : at + 1, :] = values


def shifted(block, axis, distance):
    size = math.prod(lax.axis_size(name) for name in axis)
    return lax.ppermute(block, axis, [((i - distance) % size, i) for i in range(size)])


def across(block):
    return lax.ppermute(block, "core", [(0, 1), (1, 0)])


def row_order(sizes, width):
    ids = np.arange(math.prod(sizes.values())).reshape([sizes[name] for name in AXES])
    ids = ids[..., 0].transpose(2, 0, 1, 3).reshape(sizes["x"], -1)
    per_project, per_output = 3 * width // (2 * ids.size), width // (2 * ids.size)

    def rows(per):
        return (ids[:, None, :] * per + np.arange(per)[None, :, None]).reshape(-1, 1)

    per_core = np.array([[per_project, per_output]], np.int32)
    return rows(per_project).astype(np.int32), rows(per_output).astype(np.int32), per_core


def body(features, cotangent, gain, weight, output_weight, neighbours, live, send_rows):
    rows, width = features.shape
    cap = send_rows.shape[1]
    sizes = {name: lax.axis_size(name) for name in AXES}
    devices = math.prod(sizes.values())
    scale = float(rows * devices) ** -0.5
    gain = gain.reshape(1, width)
    band = shape(cap, 2 * width)
    first, key_values, *bands = call(
        keys_kernel,
        (shape(rows, width), shape(rows, 2 * width), band, band, band, band),
        (features, gain, weight, send_rows),
        3,
    )
    steps = ((TENSOR, 1), (TENSOR, -1), (CELLS, 1), (CELLS, -1))
    received = [shifted(rows_, *step) for rows_, step in zip(bands, steps)]
    queries, grad_mixed, counts = call(
        queries_kernel,
        (shape(rows, width), shape(rows, width), shape(rows, rows + 4 * cap, dtype=F32)),
        (first, weight, output_weight, cotangent, neighbours, live),
        5,
    )
    sent, own, *backs = call(
        attention_kernel,
        (shape(rows, 4 * width), shape(rows, 2 * width, dtype=F32), band, band, band, band),
        (queries, key_values, *received, grad_mixed, counts, first, cotangent),
        8,
        scratch=(
            pltpu.VMEM((rows + 4 * cap, 2 * width), BF16),
            pltpu.VMEM((rows + 4 * cap, 2 * width), F32),
        ),
    )
    returned = [shifted(rows_, axis, -step) for rows_, (axis, step) in zip(backs, steps)]
    partner = across(sent)
    layer_output = call(
        layer_kernel, shape(rows, width), (features, sent, output_weight), 3
    )
    feature_of, cell_of, per_core = row_order(sizes, width)
    core = lax.axis_index("core").astype(jnp.int32).reshape(1, 1)

    def chosen(core_, per_, *refs):
        sent_, partner_, feature_, cell_, left_, out_ = refs
        chosen_kernel(core_, sent_, partner_, feature_, cell_, per_, left_, out_)

    left, grad_output = call(
        chosen,
        (shape(3 * width // 2, 6 * rows), shape(width // 2, width, dtype=F32)),
        (core, per_core, sent, partner, feature_of, cell_of),
        4,
        scalars=2,
    )
    near = sizes["x"]
    grad_output = lax.all_to_all(
        grad_output.reshape(near, -1, width), "x", 0, 0, tiled=True
    )
    grad_keys_values = call(
        merge_kernel, shape(rows, 2 * width), (own, *returned, send_rows), 2
    )
    partner_grads = across(grad_keys_values)
    grad_project = call(
        project_kernel,
        shape(3 * width // 2, width, dtype=F32),
        (left, sent, partner, grad_keys_values, partner_grads),
        3,
        scratch=(pltpu.VMEM((6 * rows, width), BF16),),
    )
    grad_project = lax.all_to_all(
        grad_project.reshape(near, -1, width), "x", 0, 0, tiled=True
    )
    grad_features = call(
        features_kernel,
        shape(rows, width, dtype=F32),
        (features, cotangent, gain, sent, grad_keys_values, weight),
        3,
    )
    far = devices // (2 * near)
    each = 4 * width // devices
    parts = call(
        near_kernel, shape(far, each, width, dtype=F32), (grad_project, grad_output), 2
    )
    parts = lax.all_to_all(parts, FAR, 0, 0, tiled=True)
    lanes = 128

    def far_sum(*refs):
        far_kernel(scale, *refs)

    grad_project, grad_output = call(
        far_sum,
        (
            shape(3 * width * width // devices // lanes, lanes, dtype=F32),
            shape(width * width // devices // lanes, lanes, dtype=F32),
        ),
        (parts,),
        2,
    )
    return layer_output, grad_features, grad_project.reshape(-1), grad_output.reshape(-1)


def split_mesh(mesh):
    if mesh.devices.size == 512:
        sizes = (2, 8, 4, 4, 2)
    else:
        sizes = (1, 2, mesh.devices.shape[0] // 2, mesh.devices.shape[1] // 2, 2)
    return Mesh(mesh.devices.reshape(sizes), AXES)


def solution(mesh):
    mesh = split_mesh(mesh)
    by_cell = P(AXES, None)
    return jax.shard_map(
        body,
        mesh=mesh,
        in_specs=(by_cell, by_cell, P(), P(), P(), by_cell, by_cell, by_cell),
        out_specs=(by_cell, by_cell, P(AXES), P(AXES)),
        check_vma=False,
    )
```

```python
import math

import jax
import jax.numpy as jnp
import numpy as np
from jax import lax
from jax.experimental import pallas as pl
from jax.experimental.pallas import tpu as pltpu
from jax.sharding import Mesh
from jax.sharding import PartitionSpec as P

HEADS = 8
HEAD_DIM = 64
EPSILON = 1e-06
VMEM_BYTES = 16 * 1024 * 1024
F32 = jnp.float32
BF16 = jnp.bfloat16
AXES = ("yh", "z", "x", "yl", "core")
CELLS = ("yh", "z", "x")
TENSOR = ("yl", "core")
FAR = ("yh", "z", "yl")


def dot(a, b, dims=((1,), (0,))):
    return lax.dot_general(a, b, (dims, ((), ())), preferred_element_type=F32)


def split(values):
    high = values.astype(BF16)
    return high, (values - high.astype(F32)).astype(BF16)


def call(kernel, out_shapes, args, us, scalars=0, moved=0, scratch=()):
    held = len(args) - moved
    specs = [pl.BlockSpec(memory_space=pltpu.SMEM)] * scalars
    specs += [pl.BlockSpec(memory_space=pltpu.VMEM)] * (held - scalars)
    specs += [pl.BlockSpec(memory_space=pl.ANY)] * moved
    scratch = list(scratch)
    if moved:
        scratch += [pltpu.VMEM(arg.shape, arg.dtype) for arg in args[held:]]
        scratch.append(pltpu.SemaphoreType.DMA((moved,)))

    def moving(*refs):
        away, local, arrived = refs[held : len(args)], refs[-1 - moved : -1], refs[-1]
        copies = [
            pltpu.make_async_copy(away[index], local[index], arrived.at[index])
            for index in range(moved)
        ]
        for copy in copies:
            copy.start()
        for copy in copies:
            copy.wait()
        kernel(*refs[:held], *local, *refs[len(args) : -1 - moved])

    return pl.pallas_call(
        moving if moved else kernel,
        out_shape=out_shapes,
        in_specs=specs,
        out_specs=jax.tree.map(lambda _: pl.BlockSpec(memory_space=pltpu.VMEM), out_shapes),
        scratch_shapes=scratch,
        compiler_params=pltpu.CompilerParams(vmem_limit_bytes=VMEM_BYTES),
        cost_estimate=pl.CostEstimate(
            flops=int(us * 4e8), bytes_accessed=int(us * 1e6), transcendentals=0
        ),
    )(*args)


def shape(*dims, dtype=BF16):
    return jax.ShapeDtypeStruct(dims, dtype)


def norm_factor(values):
    return lax.rsqrt(jnp.mean(values * values, axis=-1, keepdims=True) + EPSILON)


def listed(places, send_rows, index, rows):
    first = 2 * (index // 2)
    at_even, at_odd = first + index % 2, first + 1 - index % 2
    chosen = jnp.where(
        places[0, index // 2] == 0,
        send_rows[at_even : at_even + 1, :],
        send_rows[at_odd : at_odd + 1, :],
    )
    row_ids = lax.broadcasted_iota(jnp.int32, (rows, send_rows.shape[1]), 0)
    return (row_ids == chosen).astype(F32).astype(BF16)


def keys_kernel(places, features, gain, weight, send_rows, first, key_values, *bands):
    values = features[...].astype(F32)
    normed = (values * norm_factor(values) * gain[...]).astype(BF16)
    first[...] = normed
    width = weight.shape[2]
    for part in range(2):
        key_values[:, part * width : (part + 1) * width] = dot(normed, weight[1 + part]).astype(
            BF16
        )
    table = key_values[...]
    for index in range(4):
        chosen = listed(places, send_rows, index, features.shape[0])
        bands[index][...] = dot(chosen, table, ((0,), (0,))).astype(BF16)


def queries_kernel(
    places, first, weight, output_weight, cotangent, neighbours, live, queries, grad_mixed, counts
):
    queries[...] = dot(first[...], weight[0]).astype(BF16)
    grad_mixed[...] = dot(cotangent[...], output_weight[...], ((1,), (1,))).astype(BF16)
    slots = jnp.where(live[...] > 0, neighbours[...], -1)
    rows = slots.shape[1]
    cap = (counts.shape[0] - rows) // 4
    entries = lax.broadcasted_iota(jnp.int32, counts.shape, 0)
    swapped = jnp.where(
        entries < rows,
        0,
        jnp.where(entries < rows + 2 * cap, 1 - places[0, 0], 1 - places[0, 1]),
    )
    entries = jnp.bitwise_xor(entries, swapped * cap)
    total = jnp.zeros(entries.shape, F32)
    for slot in range(slots.shape[0]):
        total = total + jnp.where(slots[slot : slot + 1, :] == entries, 1.0, 0.0)
    counts[...] = total


def attention_kernel(
    queries, key_values, grad_mixed, counts, first, cotangent, band3, band1, band2, band0,
    sent, own, back1, back2, back3, table, grads,
):
    rows, width = queries.shape
    cap = band0.shape[0]
    table[:rows, :] = key_values[...]
    for index, band in enumerate((band0, band1, band2, band3)):
        start = rows + index * cap
        table[start : start + cap, :] = band[...]
    factor = HEAD_DIM**-0.5
    count = counts[...]
    is_live = count > 0
    wide = 2 * HEAD_DIM
    side = lax.broadcasted_iota(jnp.int32, (1, wide), 1) // HEAD_DIM
    down = ((0,), (0,))
    for pair in range(HEADS // 2):
        lanes = slice(pair * wide, (pair + 1) * wide)
        value_lanes = slice(width + pair * wide, width + (pair + 1) * wide)
        query, upstream = queries[:, lanes], grad_mixed[:, lanes]
        key, value = table[:, lanes], table[:, value_lanes]
        zero = jnp.zeros((), BF16)
        mixed, grad_query, grad_key, grad_value = [], [], None, None
        for half in range(2):
            mine = side == half
            query_half = jnp.where(mine, query, zero)
            upstream_half = jnp.where(mine, upstream, zero)
            scores = dot(key, query_half, ((1,), (1,))) * factor
            grad_probs = dot(value, upstream_half, ((1,), (1,)))
            scores = jnp.where(is_live, scores, -1e30)
            row_max = jnp.max(scores, axis=0, keepdims=True)
            powers = jnp.where(is_live, jnp.exp(scores - row_max), 0.0)
            probabilities = powers / jnp.sum(count * powers, axis=0, keepdims=True)
            weights = split(count * probabilities.astype(BF16).astype(F32))
            spread = count * probabilities
            grad_scores = spread * (
                grad_probs - jnp.sum(spread * grad_probs, axis=0, keepdims=True)
            )
            grad_scores = split(grad_scores * factor)
            mixed.append(sum(dot(w, value, down) for w in weights))
            grad_query.append(sum(dot(g, key, down) for g in grad_scores))
            grad_k = sum(dot(g, query_half) for g in grad_scores)
            grad_v = sum(dot(w, upstream_half) for w in weights)
            grad_key = grad_k if half == 0 else grad_key + grad_k
            grad_value = grad_v if half == 0 else grad_value + grad_v
        sent[rows : 2 * rows, lanes] = jnp.where(side == 0, mixed[0], mixed[1]).astype(BF16)
        sent[rows : 2 * rows, value_lanes] = jnp.where(
            side == 0, grad_query[0], grad_query[1]
        ).astype(BF16)
        grads[:, lanes] = grad_key
        grads[:, value_lanes] = grad_value
    own[...] = grads[:rows, :]
    sent[2 * rows :, :] = grads[rows : rows + cap, :].astype(BF16)
    for index, back in enumerate((back1, back2, back3)):
        start = rows + (index + 1) * cap
        back[...] = grads[start : start + cap, :].astype(BF16)
    sent[:rows, :width] = first[...]
    sent[:rows, width:] = cotangent[...]


def layer_kernel(features, sent, output_weight, layer_output):
    rows, width = features.shape
    mixed = sent[rows : 2 * rows, :width]
    layer_output[...] = (features[...].astype(F32) + dot(mixed, output_weight[...])).astype(BF16)


def chosen_kernel(places, per_core, sent, feature_of, cell_of, partner, left, grad_output):
    width = grad_output.shape[1]
    rows = left.shape[1] // 6
    offset = places[0, 0]
    columns = lax.broadcasted_iota(jnp.int32, (feature_of.shape[0], width), 1)
    target = feature_of[...] + offset * per_core[0, 0]
    feature = jnp.bitwise_and(target, width - 1)
    chosen = (feature == columns).astype(F32).astype(BF16)
    part = jnp.right_shift(target, width.bit_length() - 1)
    for index, source in enumerate((sent, partner)):
        picked = dot(chosen, source[:rows, :width], ((1,), (1,)))
        for piece in range(3):
            at = (2 * piece + index) * rows
            left[:, at : at + rows] = jnp.where(part == piece, picked, 0.0).astype(BF16)
    columns = lax.broadcasted_iota(jnp.int32, (cell_of.shape[0], width), 1)
    chosen = (cell_of[...] + offset * per_core[0, 1] == columns).astype(F32).astype(BF16)
    total = None
    for source in (sent, partner):
        picked = dot(chosen, source[:rows, width:], ((1,), (1,))).astype(BF16)
        product = dot(picked, source[rows : 2 * rows, :width])
        total = product if total is None else total + product
    grad_output[...] = total


def merge_kernel(places, own, send_rows, back3, back1, back2, partner, grad_keys_values):
    rows = own.shape[0]
    total = own[...]
    for index, back in enumerate((partner[2 * rows :, :], back1, back2, back3)):
        total = total + dot(listed(places, send_rows, index, rows), back[...])
    grad_keys_values[...] = total.astype(BF16)


def project_kernel(left, sent, own_grads, partner, partner_grads, grad_project, right):
    rows, width = own_grads.shape[0], grad_project.shape[1]
    for index, (early, late) in enumerate(((sent, own_grads), (partner, partner_grads))):
        pieces = (
            early[rows : 2 * rows, width:],
            late[:, :width],
            late[:, width:],
        )
        for piece in range(3):
            at = (2 * piece + index) * rows
            right[at : at + rows, :] = pieces[piece]
    grad_project[...] = dot(left[...], right[...])


def features_kernel(features, cotangent, gain, sent, late, weight, grad_features):
    rows, width = features.shape
    grad_first = dot(sent[rows : 2 * rows, width:], weight[0], ((1,), (1,)))
    for part in range(2):
        grad_first = grad_first + dot(
            late[:, part * width : (part + 1) * width], weight[1 + part], ((1,), (1,))
        )
    values = features[...].astype(F32)
    factor = norm_factor(values)
    weighted = grad_first * gain[...]
    mean = jnp.mean(values * weighted, axis=-1, keepdims=True)
    grad_features[...] = cotangent[...].astype(F32) + (
        factor * weighted - values * factor**3 * mean
    )


def near_kernel(project, output, summed):
    far = summed.shape[0]
    for source, first_row in ((project, 0), (output, summed.shape[1] - output.shape[1] // far)):
        total = source[0]
        for index in range(1, source.shape[0]):
            total = total + source[index]
        for row in range(source.shape[1] // far):
            summed[:, first_row + row, :] = total[row * far : (row + 1) * far, :]


def far_kernel(scale, parts, grad_project, grad_output):
    total = jnp.sum(parts[...], axis=0) * scale
    lanes = grad_project.shape[1]
    per_row = total.shape[1] // lanes
    project_rows = grad_project.shape[0] // per_row
    for row in range(total.shape[0]):
        for piece in range(per_row):
            values = total[row : row + 1, piece * lanes : (piece + 1) * lanes]
            if row < project_rows:
                grad_project[row * per_row + piece : row * per_row + piece + 1, :] = values
            else:
                at = (row - project_rows) * per_row + piece
                grad_output[at : at + 1, :] = values


def exchanged(block, axis, index):
    size = math.prod(lax.axis_size(name) for name in axis)
    partners = [i ^ 1 if index == 0 else ((i - 1) ^ 1) + 1 for i in range(size)]
    return lax.ppermute(block, axis, [(i, partner % size) for i, partner in enumerate(partners)])


def row_order(sizes, width):
    ids = np.arange(math.prod(sizes.values())).reshape([sizes[name] for name in AXES])
    ids = ids[..., 0].transpose(2, 0, 1, 3).reshape(sizes["x"], -1)
    per_project, per_output = 3 * width // (2 * ids.size), width // (2 * ids.size)

    def rows(per):
        return (ids[:, None, :] * per + np.arange(per)[None, :, None]).reshape(-1, 1)

    per_core = np.array([[per_project, per_output]], np.int32)
    return rows(per_project).astype(np.int32), rows(per_output).astype(np.int32), per_core


def body(features, cotangent, gain, weight, output_weight, neighbours, live, send_rows):
    rows, width = features.shape
    cap = send_rows.shape[1]
    sizes = {name: lax.axis_size(name) for name in AXES}
    devices = math.prod(sizes.values())
    scale = float(rows * devices) ** -0.5
    gain = gain.reshape(1, width)
    core = lax.axis_index("core")
    places = jnp.stack([core, lax.axis_index("x") % 2]).astype(jnp.int32).reshape(1, 2)
    band = shape(cap, 2 * width)
    first, key_values, *bands = call(
        keys_kernel,
        (shape(rows, width), shape(rows, 2 * width), band, band, band, band),
        (places, features, gain, weight, send_rows),
        3,
        scalars=1,
    )
    steps = ((TENSOR, 0), (TENSOR, 1), (CELLS, 0), (CELLS, 1))
    received = [exchanged(bands[index], *steps[index]) for index in (3, 1, 2, 0)]
    queries, grad_mixed, counts = call(
        queries_kernel,
        (shape(rows, width), shape(rows, width), shape(rows + 4 * cap, rows, dtype=F32)),
        (places, first, weight, output_weight, cotangent, neighbours.T, live.T),
        5,
        scalars=1,
    )
    sent, own, *backs = call(
        attention_kernel,
        (
            shape(2 * rows + cap, 2 * width),
            shape(rows, 2 * width, dtype=F32),
            band,
            band,
            band,
        ),
        (queries, key_values, grad_mixed, counts, first, cotangent, *received),
        8,
        moved=4,
        scratch=(
            pltpu.VMEM((rows + 4 * cap, 2 * width), BF16),
            pltpu.VMEM((rows + 4 * cap, 2 * width), F32),
        ),
    )
    returned = [exchanged(backs[index - 1], *steps[index]) for index in (3, 1, 2)]
    partner = exchanged(sent, *steps[0])
    layer_output = call(
        layer_kernel, shape(rows, width), (features, sent, output_weight), 3
    )
    feature_of, cell_of, per_core = row_order(sizes, width)
    left, grad_output = call(
        chosen_kernel,
        (shape(3 * width // 2, 6 * rows), shape(width // 2, width, dtype=F32)),
        (places, per_core, sent, feature_of, cell_of, partner),
        4,
        scalars=2,
        moved=1,
    )
    near = sizes["x"]
    grad_output = lax.all_to_all(
        grad_output.reshape(near, -1, width), "x", 0, 0, tiled=True
    )
    grad_keys_values = call(
        merge_kernel,
        shape(rows, 2 * width),
        (places, own, send_rows, *returned, partner),
        2,
        scalars=1,
        moved=4,
    )
    partner_grads = exchanged(grad_keys_values, *steps[0])
    grad_project = call(
        project_kernel,
        shape(3 * width // 2, width, dtype=F32),
        (left, sent, grad_keys_values, partner, partner_grads),
        3,
        moved=2,
        scratch=(pltpu.VMEM((6 * rows, width), BF16),),
    )
    grad_project = lax.all_to_all(
        grad_project.reshape(near, -1, width), "x", 0, 0, tiled=True
    )
    grad_features = call(
        features_kernel,
        shape(rows, width, dtype=F32),
        (features, cotangent, gain, sent, grad_keys_values, weight),
        3,
    )
    far = devices // (2 * near)
    each = 4 * width // devices
    parts = call(
        near_kernel, shape(far, each, width, dtype=F32), (grad_project, grad_output), 2, moved=2
    )
    parts = lax.all_to_all(parts, FAR, 0, 0, tiled=True)
    lanes = 128

    def far_sum(*refs):
        far_kernel(scale, *refs)

    grad_project, grad_output = call(
        far_sum,
        (
            shape(3 * width * width // devices // lanes, lanes, dtype=F32),
            shape(width * width // devices // lanes, lanes, dtype=F32),
        ),
        (parts,),
        2,
        moved=1,
    )
    return layer_output, grad_features, grad_project.reshape(-1), grad_output.reshape(-1)


def split_mesh(mesh):
    if mesh.devices.size == 512:
        sizes = (2, 8, 4, 4, 2)
    else:
        sizes = (1, 2, mesh.devices.shape[0] // 2, mesh.devices.shape[1] // 2, 2)
    return Mesh(mesh.devices.reshape(sizes), AXES)


def solution(mesh):
    mesh = split_mesh(mesh)
    by_cell = P(AXES, None)
    return jax.shard_map(
        body,
        mesh=mesh,
        in_specs=(by_cell, by_cell, P(), P(), P(), by_cell, by_cell, by_cell),
        out_specs=(by_cell, by_cell, P(AXES), P(AXES)),
        check_vma=False,
    )
```

```python
import functools
import math

import jax
import jax.numpy as jnp
import numpy as np
from jax import lax
from jax.experimental import pallas as pl
from jax.experimental.pallas import tpu as pltpu
from jax.sharding import Mesh
from jax.sharding import PartitionSpec as P

HEADS = 8
HEAD_DIM = 64
EPSILON = 1e-06
VMEM_BYTES = 16 * 1024 * 1024
F32 = jnp.float32
BF16 = jnp.bfloat16
AXES = ("yh", "z", "x", "yl", "core")
CELLS = ("yh", "z", "x")
TENSOR = ("yl", "core")
FAR = ("yh", "z", "yl")


def dot(a, b, dims=((1,), (0,))):
    return lax.dot_general(a, b, (dims, ((), ())), preferred_element_type=F32)


def split(values):
    high = values.astype(BF16)
    return high, (values - high.astype(F32)).astype(BF16)


def call(kernel, out_shapes, args, us, scalars=0, moved=0, scratch=()):
    held = len(args) - moved
    specs = [pl.BlockSpec(memory_space=pltpu.SMEM)] * scalars
    specs += [pl.BlockSpec(memory_space=pltpu.VMEM)] * (held - scalars)
    specs += [pl.BlockSpec(memory_space=pl.ANY)] * moved
    scratch = list(scratch)
    if moved:
        scratch += [pltpu.VMEM(arg.shape, arg.dtype) for arg in args[held:]]
        scratch.append(pltpu.SemaphoreType.DMA((moved,)))

    def moving(*refs):
        away, local, arrived = refs[held : len(args)], refs[-1 - moved : -1], refs[-1]
        copies = [
            pltpu.make_async_copy(away[index], local[index], arrived.at[index])
            for index in range(moved)
        ]
        for copy in copies:
            copy.start()
        for copy in copies:
            copy.wait()
        kernel(*refs[:held], *local, *refs[len(args) : -1 - moved])

    return pl.pallas_call(
        moving if moved else kernel,
        out_shape=out_shapes,
        in_specs=specs,
        out_specs=jax.tree.map(lambda _: pl.BlockSpec(memory_space=pltpu.VMEM), out_shapes),
        scratch_shapes=scratch,
        compiler_params=pltpu.CompilerParams(vmem_limit_bytes=VMEM_BYTES),
        cost_estimate=pl.CostEstimate(
            flops=int(us * 4e8), bytes_accessed=int(us * 1e6), transcendentals=0
        ),
    )(*args)


def shape(*dims, dtype=BF16):
    return jax.ShapeDtypeStruct(dims, dtype)


def norm_factor(values):
    return lax.rsqrt(jnp.mean(values * values, axis=-1, keepdims=True) + EPSILON)


def listed(places, send_rows, index, rows):
    first = 2 * (index // 2)
    at_even, at_odd = first + index % 2, first + 1 - index % 2
    chosen = jnp.where(
        places[0, index // 2] == 0,
        send_rows[at_even : at_even + 1, :],
        send_rows[at_odd : at_odd + 1, :],
    )
    row_ids = lax.broadcasted_iota(jnp.int32, (rows, send_rows.shape[1]), 0)
    return (row_ids == chosen).astype(F32).astype(BF16)


def keys_kernel(
    places, features_hbm, gain_hbm, weight_hbm, send_rows_hbm,
    first, key_values, band0, band1, band2, band3,
    features, gain, weight, send_rows, arrived,
):
    copies = [
        pltpu.make_async_copy(source, local, arrived.at[index])
        for index, (source, local) in enumerate(
            (
                (features_hbm, features),
                (gain_hbm, gain),
                (weight_hbm.at[1], weight.at[0]),
                (weight_hbm.at[2], weight.at[1]),
                (send_rows_hbm, send_rows),
            )
        )
    ]
    for copy in copies:
        copy.start()
    copies[0].wait()
    copies[1].wait()
    values = features[...].astype(F32)
    normed = (values * norm_factor(values) * gain[...]).astype(BF16)
    first[...] = normed
    width = weight.shape[2]
    for part in range(2):
        copies[2 + part].wait()
        key_values[:, part * width : (part + 1) * width] = dot(normed, weight[part]).astype(BF16)
    copies[4].wait()
    table = key_values[...]
    for index, band in enumerate((band0, band1, band2, band3)):
        chosen = listed(places, send_rows, index, features.shape[0])
        band[...] = dot(chosen, table, ((0,), (0,))).astype(BF16)


def keys_call(places, features, gain, weight, send_rows):
    rows, width = features.shape
    band = shape(send_rows.shape[1], 2 * width)
    vmem = pl.BlockSpec(memory_space=pltpu.VMEM)
    return pl.pallas_call(
        keys_kernel,
        out_shape=(shape(rows, width), shape(rows, 2 * width), band, band, band, band),
        in_specs=[pl.BlockSpec(memory_space=pltpu.SMEM)]
        + [pl.BlockSpec(memory_space=pltpu.HBM)] * 4,
        out_specs=(vmem,) * 6,
        scratch_shapes=[
            pltpu.VMEM(features.shape, BF16),
            pltpu.VMEM(gain.shape, F32),
            pltpu.VMEM((2, width, width), BF16),
            pltpu.VMEM(send_rows.shape, jnp.int32),
            pltpu.SemaphoreType.DMA((5,)),
        ],
        cost_estimate=pl.CostEstimate(
            flops=1200000000, bytes_accessed=3000000, transcendentals=0
        ),
    )(places, features, gain, weight, send_rows)


def queries_kernel(
    places, first, weight, output_weight, cotangent, neighbours, live, queries, grad_mixed, counts
):
    queries[...] = dot(first[...], weight[0]).astype(BF16)
    grad_mixed[...] = dot(cotangent[...], output_weight[...], ((1,), (1,))).astype(BF16)
    slots = jnp.where(live[...] > 0, neighbours[...], -1)
    rows = slots.shape[1]
    cap = (counts.shape[0] - rows) // 4
    entries = lax.broadcasted_iota(jnp.int32, counts.shape, 0)
    swapped = jnp.where(
        entries < rows,
        0,
        jnp.where(entries < rows + 2 * cap, 1 - places[0, 0], 1 - places[0, 1]),
    )
    entries = jnp.bitwise_xor(entries, swapped * cap)
    total = jnp.zeros(entries.shape, F32)
    for slot in range(slots.shape[0]):
        total = total + jnp.where(slots[slot : slot + 1, :] == entries, 1.0, 0.0)
    counts[...] = total


def attention_kernel(
    queries, key_values, grad_mixed, counts, first, cotangent, band3, band1, band2, band0,
    sent, own, back1, back2, back3, table, grads,
):
    rows, width = queries.shape
    cap = band0.shape[0]
    table[:rows, :] = key_values[...]
    for index, band in enumerate((band0, band1, band2, band3)):
        start = rows + index * cap
        table[start : start + cap, :] = band[...]
    factor = HEAD_DIM**-0.5
    count = counts[...]
    is_live = count > 0
    wide = 2 * HEAD_DIM
    side = lax.broadcasted_iota(jnp.int32, (1, wide), 1) // HEAD_DIM
    down = ((0,), (0,))
    for pair in range(HEADS // 2):
        lanes = slice(pair * wide, (pair + 1) * wide)
        value_lanes = slice(width + pair * wide, width + (pair + 1) * wide)
        query, upstream = queries[:, lanes], grad_mixed[:, lanes]
        key, value = table[:, lanes], table[:, value_lanes]
        zero = jnp.zeros((), BF16)
        mixed, grad_query, grad_key, grad_value = [], [], None, None
        for half in range(2):
            mine = side == half
            query_half = jnp.where(mine, query, zero)
            upstream_half = jnp.where(mine, upstream, zero)
            scores = dot(key, query_half, ((1,), (1,))) * factor
            grad_probs = dot(value, upstream_half, ((1,), (1,)))
            scores = jnp.where(is_live, scores, -1e30)
            row_max = jnp.max(scores, axis=0, keepdims=True)
            powers = jnp.where(is_live, jnp.exp(scores - row_max), 0.0)
            probabilities = powers / jnp.sum(count * powers, axis=0, keepdims=True)
            weights = split(count * probabilities.astype(BF16).astype(F32))
            spread = count * probabilities
            grad_scores = spread * (
                grad_probs - jnp.sum(spread * grad_probs, axis=0, keepdims=True)
            )
            grad_scores = split(grad_scores * factor)
            mixed.append(sum(dot(w, value, down) for w in weights))
            grad_query.append(sum(dot(g, key, down) for g in grad_scores))
            grad_k = sum(dot(g, query_half) for g in grad_scores)
            grad_v = sum(dot(w, upstream_half) for w in weights)
            grad_key = grad_k if half == 0 else grad_key + grad_k
            grad_value = grad_v if half == 0 else grad_value + grad_v
        sent[rows : 2 * rows, lanes] = jnp.where(side == 0, mixed[0], mixed[1]).astype(BF16)
        sent[rows : 2 * rows, value_lanes] = jnp.where(
            side == 0, grad_query[0], grad_query[1]
        ).astype(BF16)
        grads[:, lanes] = grad_key
        grads[:, value_lanes] = grad_value
    own[...] = grads[:rows, :]
    sent[2 * rows :, :] = grads[rows : rows + cap, :].astype(BF16)
    for index, back in enumerate((back1, back2, back3)):
        start = rows + (index + 1) * cap
        back[...] = grads[start : start + cap, :].astype(BF16)
    sent[:rows, :width] = first[...]
    sent[:rows, width:] = cotangent[...]


def layer_kernel(features, sent, output_weight, layer_output):
    rows, width = features.shape
    mixed = sent[rows : 2 * rows, :width]
    layer_output[...] = (features[...].astype(F32) + dot(mixed, output_weight[...])).astype(BF16)


def chosen_kernel(places, per_core, sent, feature_of, cell_of, partner, left, grad_output):
    width, rows = sent.shape[1] // 2, left.shape[1] // 6
    columns = lax.broadcasted_iota(jnp.int32, (feature_of.shape[0], width), 1)
    target = feature_of[...] + places[0, 0] * per_core[0, 0]
    feature = jnp.bitwise_and(target, width - 1)
    chosen = (feature == columns).astype(F32).astype(BF16)
    part = jnp.right_shift(target, width.bit_length() - 1)
    for index, source in enumerate((sent, partner)):
        picked = dot(chosen, source[:rows, :width], ((1,), (1,)))
        for piece in range(3):
            at = (2 * piece + index) * rows
            left[:, at : at + rows] = jnp.where(part == piece, picked, 0.0).astype(BF16)
    columns = lax.broadcasted_iota(jnp.int32, (cell_of.shape[0], width), 1)
    target = cell_of[...] + places[0, 0] * per_core[0, 1]
    chosen = (target == columns).astype(F32).astype(BF16)
    total = None
    for source in (sent, partner):
        picked = dot(chosen, source[:rows, width:], ((1,), (1,))).astype(BF16)
        product = dot(picked, source[rows : 2 * rows, :width])
        total = product if total is None else total + product
    grad_output[...] = total


def merge_kernel(places, own, send_rows, back3, back1, back2, partner, grad_keys_values):
    rows = own.shape[0]
    total = own[...]
    for index, back in enumerate((partner[2 * rows :, :], back1, back2, back3)):
        total = total + dot(listed(places, send_rows, index, rows), back[...])
    grad_keys_values[...] = total.astype(BF16)


def project_kernel(
    left, sent, own_grads, grad_output, partner, partner_grads, both, right
):
    rows, width = own_grads.shape[0], both.shape[2]
    for index, (early, late) in enumerate(((sent, own_grads), (partner, partner_grads))):
        pieces = (
            early[rows : 2 * rows, width:],
            late[:, :width],
            late[:, width:],
        )
        for piece in range(3):
            at = (2 * piece + index) * rows
            right[at : at + rows, :] = pieces[piece]
    near = both.shape[0]
    count = left.shape[0] // near
    for index in range(near):
        both[index, :count, :] = dot(left[index * count : (index + 1) * count, :], right[...])
    count = grad_output.shape[0] // near
    for index in range(near):
        both[index, -count:, :] = grad_output[index * count : (index + 1) * count, :]


def features_kernel(features, cotangent, gain, sent, late, weight, grad_features):
    rows, width = features.shape
    grad_first = dot(sent[rows : 2 * rows, width:], weight[0], ((1,), (1,)))
    for part in range(2):
        grad_first = grad_first + dot(
            late[:, part * width : (part + 1) * width], weight[1 + part], ((1,), (1,))
        )
    values = features[...].astype(F32)
    factor = norm_factor(values)
    weighted = grad_first * gain[...]
    mean = jnp.mean(values * weighted, axis=-1, keepdims=True)
    grad_features[...] = cotangent[...].astype(F32) + (
        factor * weighted - values * factor**3 * mean
    )


def near_kernel(both, summed):
    far = summed.shape[0]
    total = both[0]
    for index in range(1, both.shape[0]):
        total = total + both[index]
    for row in range(summed.shape[1]):
        summed[:, row, :] = total[row * far : (row + 1) * far, :]


def far_kernel(scale, parts, grad_project, grad_output):
    total = jnp.sum(parts[...], axis=0) * scale
    lanes = grad_project.shape[1]
    per_row = total.shape[1] // lanes
    project_rows = grad_project.shape[0] // per_row
    for row in range(total.shape[0]):
        for piece in range(per_row):
            values = total[row : row + 1, piece * lanes : (piece + 1) * lanes]
            if row < project_rows:
                at = row * per_row + piece
                grad_project[at : at + 1, :] = values
            else:
                at = (row - project_rows) * per_row + piece
                grad_output[at : at + 1, :] = values


def exchanged(block, axis, index):
    size = math.prod(lax.axis_size(name) for name in axis)
    partners = [i ^ 1 if index == 0 else ((i - 1) ^ 1) + 1 for i in range(size)]
    return lax.ppermute(block, axis, [(i, partner % size) for i, partner in enumerate(partners)])


def row_order(sizes, width):
    ids = np.arange(math.prod(sizes.values())).reshape([sizes[name] for name in AXES])
    ids = ids[..., 0].transpose(2, 0, 1, 3).reshape(sizes["x"], -1)
    per_project, per_output = 3 * width // (2 * ids.size), width // (2 * ids.size)

    def rows(per):
        return (ids[:, None, :] * per + np.arange(per)[None, :, None]).reshape(-1, 1)

    per_core = np.array([[per_project, per_output]], np.int32)
    return rows(per_project).astype(np.int32), rows(per_output).astype(np.int32), per_core


def body(features, cotangent, gain, weight, output_weight, neighbours, live, send_rows):
    rows, width = features.shape
    cap = send_rows.shape[1]
    sizes = {name: lax.axis_size(name) for name in AXES}
    devices = math.prod(sizes.values())
    scale = float(rows * devices) ** -0.5
    gain = gain.reshape(1, width)
    core = lax.axis_index("core")
    places = jnp.stack([core, lax.axis_index("x") % 2]).astype(jnp.int32).reshape(1, 2)
    band = shape(cap, 2 * width)
    first, key_values, *bands = keys_call(places, features, gain, weight, send_rows)
    steps = ((TENSOR, 0), (TENSOR, 1), (CELLS, 0), (CELLS, 1))
    received = [exchanged(bands[index], *steps[index]) for index in (3, 1, 2, 0)]
    queries, grad_mixed, counts = call(
        queries_kernel,
        (shape(rows, width), shape(rows, width), shape(rows + 4 * cap, rows, dtype=F32)),
        (places, first, weight, output_weight, cotangent, neighbours.T, live.T),
        5,
        scalars=1,
    )
    sent, own, *backs = call(
        attention_kernel,
        (
            shape(2 * rows + cap, 2 * width),
            shape(rows, 2 * width, dtype=F32),
            band,
            band,
            band,
        ),
        (queries, key_values, grad_mixed, counts, first, cotangent, *received),
        8,
        moved=4,
        scratch=(
            pltpu.VMEM((rows + 4 * cap, 2 * width), BF16),
            pltpu.VMEM((rows + 4 * cap, 2 * width), F32),
        ),
    )
    returned = [exchanged(backs[index - 1], *steps[index]) for index in (3, 1, 2)]
    partner = exchanged(sent, *steps[0])
    layer_output = call(
        layer_kernel, shape(rows, width), (features, sent, output_weight), 3
    )
    feature_of, cell_of, per_core = row_order(sizes, width)
    near = sizes["x"]
    far = devices // (2 * near)
    left, grad_output = call(
        chosen_kernel,
        (shape(3 * width // 2, 6 * rows), shape(width // 2, width, dtype=F32)),
        (places, per_core, sent, feature_of, cell_of, partner),
        3,
        scalars=2,
        moved=1,
    )
    grad_keys_values = call(
        merge_kernel,
        shape(rows, 2 * width),
        (places, own, send_rows, *returned, partner),
        2,
        scalars=1,
        moved=4,
    )
    partner_grads = exchanged(grad_keys_values, *steps[0])
    both = call(
        project_kernel,
        shape(near, 2 * width // near, width, dtype=F32),
        (left, sent, grad_keys_values, grad_output, partner, partner_grads),
        3,
        moved=2,
        scratch=(pltpu.VMEM((6 * rows, width), BF16),),
    )
    both = lax.all_to_all(both, "x", 0, 0, tiled=True)
    grad_features = call(
        features_kernel,
        shape(rows, width, dtype=F32),
        (features, cotangent, gain, sent, grad_keys_values, weight),
        3,
    )
    parts = call(
        near_kernel, shape(far, 4 * width // devices, width, dtype=F32), (both,), 2, moved=1
    )
    parts = lax.all_to_all(parts, FAR, 0, 0, tiled=True)
    grad_project, grad_output = call(
        functools.partial(far_kernel, scale),
        tuple(shape(count * width * width // devices // 128, 128, dtype=F32) for count in (3, 1)),
        (parts,),
        2,
        moved=1,
    )
    return layer_output, grad_features, grad_project.reshape(-1), grad_output.reshape(-1)


def split_mesh(mesh):
    if mesh.devices.size == 512:
        sizes = (2, 8, 4, 4, 2)
    else:
        sizes = (1, 2, mesh.devices.shape[0] // 2, mesh.devices.shape[1] // 2, 2)
    return Mesh(mesh.devices.reshape(sizes), AXES)


def solution(mesh):
    mesh = split_mesh(mesh)
    by_cell = P(AXES, None)
    return jax.shard_map(
        body,
        mesh=mesh,
        in_specs=(by_cell, by_cell, P(), P(), P(), by_cell, by_cell, by_cell),
        out_specs=(by_cell, by_cell, P(AXES), P(AXES)),
        check_vma=False,
    )
```

```python
import functools
import math

import jax
import jax.numpy as jnp
import numpy as np
from jax import lax
from jax.experimental import pallas as pl
from jax.experimental.pallas import tpu as pltpu
from jax.sharding import Mesh
from jax.sharding import PartitionSpec as P

HEADS = 8
HEAD_DIM = 64
EPSILON = 1e-06
HEADER = 16
HEADROOM = 13.0
VMEM_BYTES = 16 * 1024 * 1024
F32 = jnp.float32
BF16 = jnp.bfloat16
AXES = ("yh", "z", "x", "yl", "core")
CELLS = ("yh", "z", "x")
TENSOR = ("yl", "core")
FAR = ("yh", "z", "yl")


def dot(a, b, dims=((1,), (0,))):
    return lax.dot_general(a, b, (dims, ((), ())), preferred_element_type=F32)


def split(values):
    high = values.astype(BF16)
    return high, (values - high.astype(F32)).astype(BF16)


def call(kernel, out_shapes, args, us, scalars=0, moved=0, scratch=()):
    held = len(args) - moved
    specs = [pl.BlockSpec(memory_space=pltpu.SMEM)] * scalars
    specs += [pl.BlockSpec(memory_space=pltpu.VMEM)] * (held - scalars)
    specs += [pl.BlockSpec(memory_space=pl.ANY)] * moved
    scratch = list(scratch)
    if moved:
        scratch += [pltpu.VMEM(arg.shape, arg.dtype) for arg in args[held:]]
        scratch.append(pltpu.SemaphoreType.DMA((moved,)))

    def moving(*refs):
        away, local, arrived = refs[held : len(args)], refs[-1 - moved : -1], refs[-1]
        copies = [
            pltpu.make_async_copy(away[index], local[index], arrived.at[index])
            for index in range(moved)
        ]
        for copy in copies:
            copy.start()
        for copy in copies:
            copy.wait()
        kernel(*refs[:held], *local, *refs[len(args) : -1 - moved])

    return pl.pallas_call(
        moving if moved else kernel,
        out_shape=out_shapes,
        in_specs=specs,
        out_specs=jax.tree.map(lambda _: pl.BlockSpec(memory_space=pltpu.VMEM), out_shapes),
        scratch_shapes=scratch,
        compiler_params=pltpu.CompilerParams(vmem_limit_bytes=VMEM_BYTES),
        cost_estimate=pl.CostEstimate(
            flops=int(us * 4e8), bytes_accessed=int(us * 1e6), transcendentals=0
        ),
    )(*args)


def shape(*dims, dtype=BF16):
    return jax.ShapeDtypeStruct(dims, dtype)


def norm_factor(values):
    return lax.rsqrt(jnp.mean(values * values, axis=-1, keepdims=True) + EPSILON)


def listed(places, send_rows, index, rows):
    first = 2 * (index // 2)
    at_even, at_odd = first + index % 2, first + 1 - index % 2
    chosen = jnp.where(
        places[0, index // 2] == 0,
        send_rows[at_even : at_even + 1, :],
        send_rows[at_odd : at_odd + 1, :],
    )
    row_ids = lax.broadcasted_iota(jnp.int32, (rows, send_rows.shape[1]), 0)
    return (row_ids == chosen).astype(F32).astype(BF16)


def keys_kernel(
    places, features_hbm, gain_hbm, weight_hbm, send_rows_hbm,
    first, key_values, band0, band1, band2, band3,
    features, gain, weight, send_rows, arrived,
):
    copies = [
        pltpu.make_async_copy(source, local, arrived.at[index])
        for index, (source, local) in enumerate(
            (
                (features_hbm, features),
                (gain_hbm, gain),
                (weight_hbm.at[1], weight.at[0]),
                (weight_hbm.at[2], weight.at[1]),
                (send_rows_hbm, send_rows),
            )
        )
    ]
    for copy in copies:
        copy.start()
    copies[0].wait()
    copies[1].wait()
    values = features[...].astype(F32)
    normed = (values * norm_factor(values) * gain[...]).astype(BF16)
    first[...] = normed
    width = weight.shape[2]
    for part in range(2):
        copies[2 + part].wait()
        key_values[:, part * width : (part + 1) * width] = dot(normed, weight[part]).astype(BF16)
    copies[4].wait()
    table = key_values[...]
    for index, band in enumerate((band0, band1, band2, band3)):
        chosen = listed(places, send_rows, index, features.shape[0])
        band[...] = dot(chosen, table, ((0,), (0,))).astype(BF16)


def keys_call(places, features, gain, weight, send_rows):
    rows, width = features.shape
    band = shape(send_rows.shape[1], 2 * width)
    vmem = pl.BlockSpec(memory_space=pltpu.VMEM)
    return pl.pallas_call(
        keys_kernel,
        out_shape=(shape(rows, width), shape(rows, 2 * width), band, band, band, band),
        in_specs=[pl.BlockSpec(memory_space=pltpu.SMEM)]
        + [pl.BlockSpec(memory_space=pltpu.HBM)] * 4,
        out_specs=(vmem,) * 6,
        scratch_shapes=[
            pltpu.VMEM(features.shape, BF16),
            pltpu.VMEM(gain.shape, F32),
            pltpu.VMEM((2, width, width), BF16),
            pltpu.VMEM(send_rows.shape, jnp.int32),
            pltpu.SemaphoreType.DMA((5,)),
        ],
        cost_estimate=pl.CostEstimate(
            flops=1200000000, bytes_accessed=3000000, transcendentals=0
        ),
    )(places, features, gain, weight, send_rows)


def queries_kernel(
    places, first, weight, output_weight, cotangent, neighbours, live, queries, grad_mixed, counts
):
    queries[...] = dot(first[...], weight[0]).astype(BF16)
    grad_mixed[...] = dot(cotangent[...], output_weight[...], ((1,), (1,))).astype(BF16)
    slots = jnp.where(live[...] > 0, neighbours[...], -1)
    rows = slots.shape[1]
    cap = (counts.shape[0] - rows) // 4
    entries = lax.broadcasted_iota(jnp.int32, counts.shape, 0)
    swapped = jnp.where(
        entries < rows,
        0,
        jnp.where(entries < rows + 2 * cap, 1 - places[0, 0], 1 - places[0, 1]),
    )
    entries = jnp.bitwise_xor(entries, swapped * cap)
    total = jnp.zeros(entries.shape, F32)
    for slot in range(slots.shape[0]):
        total = total + jnp.where(slots[slot : slot + 1, :] == entries, 1.0, 0.0)
    counts[...] = total


def attention_kernel(
    queries, key_values, grad_mixed, counts, first, cotangent, band3, band1, band2, band0,
    sent, own, back1, back2, back3, table, grads,
):
    rows, width = queries.shape
    cap = band0.shape[0]
    table[:rows, :] = key_values[...]
    for index, band in enumerate((band0, band1, band2, band3)):
        start = rows + index * cap
        table[start : start + cap, :] = band[...]
    factor = HEAD_DIM**-0.5
    count = counts[...]
    is_live = count > 0
    wide = 2 * HEAD_DIM
    side = lax.broadcasted_iota(jnp.int32, (1, wide), 1) // HEAD_DIM
    down = ((0,), (0,))
    for pair in range(HEADS // 2):
        lanes = slice(pair * wide, (pair + 1) * wide)
        value_lanes = slice(width + pair * wide, width + (pair + 1) * wide)
        query, upstream = queries[:, lanes], grad_mixed[:, lanes]
        key, value = table[:, lanes], table[:, value_lanes]
        zero = jnp.zeros((), BF16)
        mixed, grad_query, grad_key, grad_value = [], [], None, None
        for half in range(2):
            mine = side == half
            query_half = jnp.where(mine, query, zero)
            upstream_half = jnp.where(mine, upstream, zero)
            scores = dot(key, query_half, ((1,), (1,))) * factor
            grad_probs = dot(value, upstream_half, ((1,), (1,)))
            scores = jnp.where(is_live, scores, -1e30)
            row_max = jnp.max(scores, axis=0, keepdims=True)
            powers = jnp.where(is_live, jnp.exp(scores - row_max), 0.0)
            probabilities = powers / jnp.sum(count * powers, axis=0, keepdims=True)
            weights = split(count * probabilities.astype(BF16).astype(F32))
            spread = count * probabilities
            grad_scores = spread * (
                grad_probs - jnp.sum(spread * grad_probs, axis=0, keepdims=True)
            )
            grad_scores = split(grad_scores * factor)
            mixed.append(sum(dot(w, value, down) for w in weights))
            grad_query.append(sum(dot(g, key, down) for g in grad_scores))
            grad_k = sum(dot(g, query_half) for g in grad_scores)
            grad_v = sum(dot(w, upstream_half) for w in weights)
            grad_key = grad_k if half == 0 else grad_key + grad_k
            grad_value = grad_v if half == 0 else grad_value + grad_v
        sent[rows : 2 * rows, lanes] = jnp.where(side == 0, mixed[0], mixed[1]).astype(BF16)
        sent[rows : 2 * rows, value_lanes] = jnp.where(
            side == 0, grad_query[0], grad_query[1]
        ).astype(BF16)
        grads[:, lanes] = grad_key
        grads[:, value_lanes] = grad_value
    own[...] = grads[:rows, :]
    sent[2 * rows :, :] = grads[rows : rows + cap, :].astype(BF16)
    for index, back in enumerate((back1, back2, back3)):
        start = rows + (index + 1) * cap
        back[...] = grads[start : start + cap, :].astype(BF16)
    sent[:rows, :width] = first[...]
    sent[:rows, width:] = cotangent[...]


def layer_kernel(features, sent, output_weight, layer_output):
    rows, width = features.shape
    mixed = sent[rows : 2 * rows, :width]
    layer_output[...] = (features[...].astype(F32) + dot(mixed, output_weight[...])).astype(BF16)


def chosen_kernel(places, per_core, sent, feature_of, cell_of, partner, left, grad_output):
    width, rows = sent.shape[1] // 2, left.shape[1] // 6
    columns = lax.broadcasted_iota(jnp.int32, (feature_of.shape[0], width), 1)
    target = feature_of[...] + places[0, 0] * per_core[0, 0]
    feature = jnp.bitwise_and(target, width - 1)
    chosen = (feature == columns).astype(F32).astype(BF16)
    part = jnp.right_shift(target, width.bit_length() - 1)
    for index, source in enumerate((sent, partner)):
        picked = dot(chosen, source[:rows, :width], ((1,), (1,)))
        for piece in range(3):
            at = (2 * piece + index) * rows
            left[:, at : at + rows] = jnp.where(part == piece, picked, 0.0).astype(BF16)
    columns = lax.broadcasted_iota(jnp.int32, (cell_of.shape[0], width), 1)
    target = cell_of[...] + places[0, 0] * per_core[0, 1]
    chosen = (target == columns).astype(F32).astype(BF16)
    total = None
    for source in (sent, partner):
        picked = dot(chosen, source[:rows, width:], ((1,), (1,))).astype(BF16)
        product = dot(picked, source[rows : 2 * rows, :width])
        total = product if total is None else total + product
    grad_output[...] = total


def merge_kernel(places, own, send_rows, back3, back1, back2, partner, grad_keys_values):
    rows = own.shape[0]
    total = own[...]
    for index, back in enumerate((partner[2 * rows :, :], back1, back2, back3)):
        total = total + dot(listed(places, send_rows, index, rows), back[...])
    grad_keys_values[...] = total.astype(BF16)


def exponent(values):
    largest = jnp.max(jnp.max(jnp.abs(values), axis=0, keepdims=True), axis=1, keepdims=True)
    return jnp.floor(jnp.log2(jnp.maximum(largest, 1e-30)))


def project_kernel(left, sent, own_grads, grad_output, partner, partner_grads, both, right):
    rows, width = own_grads.shape[0], both.shape[2]
    for index, (early, late) in enumerate(((sent, own_grads), (partner, partner_grads))):
        pieces = (
            early[rows : 2 * rows, width:],
            late[:, :width],
            late[:, width:],
        )
        for piece in range(3):
            at = (2 * piece + index) * rows
            right[at : at + rows, :] = pieces[piece]
    near = both.shape[0]
    first_row = 0
    for part, values in enumerate((dot(left[...], right[...]), grad_output[...])):
        power = exponent(values)
        scaled = values * jnp.exp2(HEADROOM - power)
        count = values.shape[0] // near
        at = both.shape[1] - HEADER + part * (HEADER // 2)
        for index in range(near):
            both[index, first_row : first_row + count, :] = scaled[
                index * count : (index + 1) * count, :
            ]
            both[index, at : at + HEADER // 2, :] = jnp.broadcast_to(power, (HEADER // 2, width))
        first_row += count


def features_kernel(features, cotangent, gain, sent, late, weight, grad_features):
    rows, width = features.shape
    grad_first = dot(sent[rows : 2 * rows, width:], weight[0], ((1,), (1,)))
    for part in range(2):
        grad_first = grad_first + dot(
            late[:, part * width : (part + 1) * width], weight[1 + part], ((1,), (1,))
        )
    values = features[...].astype(F32)
    factor = norm_factor(values)
    weighted = grad_first * gain[...]
    mean = jnp.mean(values * weighted, axis=-1, keepdims=True)
    grad_features[...] = cotangent[...].astype(F32) + (
        factor * weighted - values * factor**3 * mean
    )


def near_kernel(both, summed):
    far, each = summed.shape[:2]
    first_row = 0
    for part, per in enumerate((each - each // 4, each // 4)):
        at = both.shape[1] - HEADER + part * (HEADER // 2)
        total = None
        for index in range(both.shape[0]):
            scale = jnp.exp2(both[index, at : at + 1, :] - HEADROOM)
            values = both[index, first_row * far : (first_row + per) * far, :] * scale
            total = values if total is None else total + values
        for row in range(per):
            summed[:, first_row + row, :] = total[row * far : (row + 1) * far, :]
        first_row += per


def far_kernel(scale, parts, grad_project, grad_output):
    total = jnp.sum(parts[...], axis=0) * scale
    lanes = grad_project.shape[1]
    per_row = total.shape[1] // lanes
    project_rows = grad_project.shape[0] // per_row
    for row in range(total.shape[0]):
        for piece in range(per_row):
            values = total[row : row + 1, piece * lanes : (piece + 1) * lanes]
            if row < project_rows:
                at = row * per_row + piece
                grad_project[at : at + 1, :] = values
            else:
                at = (row - project_rows) * per_row + piece
                grad_output[at : at + 1, :] = values


def exchanged(block, axis, index):
    size = math.prod(lax.axis_size(name) for name in axis)
    partners = [i ^ 1 if index == 0 else ((i - 1) ^ 1) + 1 for i in range(size)]
    return lax.ppermute(block, axis, [(i, partner % size) for i, partner in enumerate(partners)])


def row_order(sizes, width):
    ids = np.arange(math.prod(sizes.values())).reshape([sizes[name] for name in AXES])
    ids = ids[..., 0].transpose(2, 0, 1, 3).reshape(sizes["x"], -1)
    per_project, per_output = 3 * width // (2 * ids.size), width // (2 * ids.size)

    def rows(per):
        return (ids[:, None, :] * per + np.arange(per)[None, :, None]).reshape(-1, 1)

    per_core = np.array([[per_project, per_output]], np.int32)
    return rows(per_project).astype(np.int32), rows(per_output).astype(np.int32), per_core


def body(features, cotangent, gain, weight, output_weight, neighbours, live, send_rows):
    rows, width = features.shape
    cap = send_rows.shape[1]
    sizes = {name: lax.axis_size(name) for name in AXES}
    devices = math.prod(sizes.values())
    scale = float(rows * devices) ** -0.5
    gain = gain.reshape(1, width)
    core = lax.axis_index("core")
    places = jnp.stack([core, lax.axis_index("x") % 2]).astype(jnp.int32).reshape(1, 2)
    band = shape(cap, 2 * width)
    first, key_values, *bands = keys_call(places, features, gain, weight, send_rows)
    steps = ((TENSOR, 0), (TENSOR, 1), (CELLS, 0), (CELLS, 1))
    received = [exchanged(bands[index], *steps[index]) for index in (3, 1, 2, 0)]
    queries, grad_mixed, counts = call(
        queries_kernel,
        (shape(rows, width), shape(rows, width), shape(rows + 4 * cap, rows, dtype=F32)),
        (places, first, weight, output_weight, cotangent, neighbours.T, live.T),
        5,
        scalars=1,
    )
    sent, own, *backs = call(
        attention_kernel,
        (
            shape(2 * rows + cap, 2 * width),
            shape(rows, 2 * width, dtype=F32),
            band,
            band,
            band,
        ),
        (queries, key_values, grad_mixed, counts, first, cotangent, *received),
        8,
        moved=4,
        scratch=(
            pltpu.VMEM((rows + 4 * cap, 2 * width), BF16),
            pltpu.VMEM((rows + 4 * cap, 2 * width), F32),
        ),
    )
    returned = [exchanged(backs[index - 1], *steps[index]) for index in (3, 1, 2)]
    partner = exchanged(sent, *steps[0])
    layer_output = call(
        layer_kernel, shape(rows, width), (features, sent, output_weight), 3
    )
    feature_of, cell_of, per_core = row_order(sizes, width)
    near = sizes["x"]
    far = devices // (2 * near)
    left, grad_output = call(
        chosen_kernel,
        (shape(3 * width // 2, 6 * rows), shape(width // 2, width, dtype=F32)),
        (places, per_core, sent, feature_of, cell_of, partner),
        3,
        scalars=2,
        moved=1,
    )
    grad_keys_values = call(
        merge_kernel,
        shape(rows, 2 * width),
        (places, own, send_rows, *returned, partner),
        2,
        scalars=1,
        moved=4,
    )
    partner_grads = exchanged(grad_keys_values, *steps[0])
    both = call(
        project_kernel,
        shape(near, 2 * width // near + HEADER, width, dtype=F32),
        (left, sent, grad_keys_values, grad_output, partner, partner_grads),
        3,
        moved=2,
        scratch=(pltpu.VMEM((6 * rows, width), BF16),),
    )
    both = lax.all_to_all(both.astype(jnp.float16), "x", 0, 0, tiled=True).astype(F32)
    grad_features = call(
        features_kernel,
        shape(rows, width, dtype=F32),
        (features, cotangent, gain, sent, grad_keys_values, weight),
        3,
    )
    parts = call(
        near_kernel, shape(far, 4 * width // devices, width, dtype=F32), (both,), 2, moved=1
    )
    parts = lax.all_to_all(parts, FAR, 0, 0, tiled=True)
    grad_project, grad_output = call(
        functools.partial(far_kernel, scale),
        tuple(shape(count * width * width // devices // 128, 128, dtype=F32) for count in (3, 1)),
        (parts,),
        2,
        moved=1,
    )
    return layer_output, grad_features, grad_project.reshape(-1), grad_output.reshape(-1)


def split_mesh(mesh):
    if mesh.devices.size == 512:
        sizes = (2, 8, 4, 4, 2)
    else:
        sizes = (1, 2, mesh.devices.shape[0] // 2, mesh.devices.shape[1] // 2, 2)
    return Mesh(mesh.devices.reshape(sizes), AXES)


def solution(mesh):
    mesh = split_mesh(mesh)
    by_cell = P(AXES, None)
    return jax.shard_map(
        body,
        mesh=mesh,
        in_specs=(by_cell, by_cell, P(), P(), P(), by_cell, by_cell, by_cell),
        out_specs=(by_cell, by_cell, P(AXES), P(AXES)),
        check_vma=False,
    )
```

```python
import functools
import math

import jax
import jax.numpy as jnp
import numpy as np
from jax import lax
from jax.experimental import pallas as pl
from jax.experimental.pallas import tpu as pltpu
from jax.sharding import Mesh
from jax.sharding import PartitionSpec as P

HEADS = 8
HEAD_DIM = 64
EPSILON = 1e-06
HEADER = 16
HEADROOM = 13.0
VMEM_BYTES = 16 * 1024 * 1024
F32 = jnp.float32
BF16 = jnp.bfloat16
AXES = ("yh", "z", "x", "yl", "core")
CELLS = ("yh", "z", "x")
TENSOR = ("yl", "core")
FAR = ("yh", "z", "yl")


def dot(a, b, dims=((1,), (0,))):
    return lax.dot_general(a, b, (dims, ((), ())), preferred_element_type=F32)


def split(values):
    high = values.astype(BF16)
    return high, (values - high.astype(F32)).astype(BF16)


def call(kernel, out_shapes, args, us, moved=0, scratch=()):
    held = len(args) - moved
    specs = [pl.BlockSpec(memory_space=pltpu.VMEM)] * held
    specs += [pl.BlockSpec(memory_space=pl.ANY)] * moved
    scratch = list(scratch)
    if moved:
        scratch += [pltpu.VMEM(arg.shape, arg.dtype) for arg in args[held:]]
        scratch.append(pltpu.SemaphoreType.DMA((moved,)))

    def moving(*refs):
        away, local, arrived = refs[held : len(args)], refs[-1 - moved : -1], refs[-1]
        copies = [
            pltpu.make_async_copy(away[index], local[index], arrived.at[index])
            for index in range(moved)
        ]
        for copy in copies:
            copy.start()
        for copy in copies:
            copy.wait()
        kernel(*refs[:held], *local, *refs[len(args) : -1 - moved])

    return pl.pallas_call(
        moving if moved else kernel,
        out_shape=out_shapes,
        in_specs=specs,
        out_specs=jax.tree.map(lambda _: pl.BlockSpec(memory_space=pltpu.VMEM), out_shapes),
        scratch_shapes=scratch,
        compiler_params=pltpu.CompilerParams(vmem_limit_bytes=VMEM_BYTES),
        cost_estimate=pl.CostEstimate(
            flops=int(us * 4e8), bytes_accessed=int(us * 1e6), transcendentals=0
        ),
    )(*args)


def shape(*dims, dtype=BF16):
    return jax.ShapeDtypeStruct(dims, dtype)


def norm_factor(values):
    return lax.rsqrt(jnp.mean(values * values, axis=-1, keepdims=True) + EPSILON)


def here():
    return lax.axis_index("core"), lax.rem(lax.axis_index("x"), 2)


def listed(places, send_rows, index, rows):
    first = 2 * (index // 2)
    at_even, at_odd = first + index % 2, first + 1 - index % 2
    chosen = jnp.where(
        places[index // 2] == 0,
        send_rows[at_even : at_even + 1, :],
        send_rows[at_odd : at_odd + 1, :],
    )
    row_ids = lax.broadcasted_iota(jnp.int32, (rows, send_rows.shape[1]), 0)
    return (row_ids == chosen).astype(F32).astype(BF16)


def keys_kernel(
    features_hbm, gain_hbm, weight_hbm, send_rows_hbm,
    first, key_values, band0, band1, band2, band3,
    features, gain, weight, send_rows, arrived,
):
    copies = [
        pltpu.make_async_copy(source, local, arrived.at[index])
        for index, (source, local) in enumerate(
            (
                (features_hbm, features),
                (gain_hbm, gain),
                (weight_hbm.at[1], weight.at[0]),
                (weight_hbm.at[2], weight.at[1]),
                (send_rows_hbm, send_rows),
            )
        )
    ]
    for copy in copies:
        copy.start()
    copies[0].wait()
    copies[1].wait()
    values = features[...].astype(F32)
    normed = (values * norm_factor(values) * gain[...]).astype(BF16)
    first[...] = normed
    width = weight.shape[2]
    for part in range(2):
        copies[2 + part].wait()
        key_values[:, part * width : (part + 1) * width] = dot(normed, weight[part]).astype(BF16)
    copies[4].wait()
    table = key_values[...]
    places = here()
    for index, band in enumerate((band0, band1, band2, band3)):
        chosen = listed(places, send_rows, index, features.shape[0])
        band[...] = dot(chosen, table, ((0,), (0,))).astype(BF16)


def keys_call(features, gain, weight, send_rows):
    rows, width = features.shape
    band = shape(send_rows.shape[1], 2 * width)
    vmem = pl.BlockSpec(memory_space=pltpu.VMEM)
    return pl.pallas_call(
        keys_kernel,
        out_shape=(shape(rows, width), shape(rows, 2 * width), band, band, band, band),
        in_specs=[pl.BlockSpec(memory_space=pltpu.HBM)] * 4,
        out_specs=(vmem,) * 6,
        scratch_shapes=[
            pltpu.VMEM(features.shape, BF16),
            pltpu.VMEM(gain.shape, F32),
            pltpu.VMEM((2, width, width), BF16),
            pltpu.VMEM(send_rows.shape, jnp.int32),
            pltpu.SemaphoreType.DMA((5,)),
        ],
        compiler_params=pltpu.CompilerParams(vmem_limit_bytes=VMEM_BYTES),
        cost_estimate=pl.CostEstimate(
            flops=1200000000, bytes_accessed=3000000, transcendentals=0
        ),
    )(
        *(
            pltpu.with_memory_space_constraint(array, pltpu.HBM)
            for array in (features, gain, weight, send_rows)
        )
    )


def queries_kernel(
    first, weight, output_weight, cotangent, neighbours, live, queries, grad_mixed, counts
):
    places = here()
    queries[...] = dot(first[...], weight[0]).astype(BF16)
    grad_mixed[...] = dot(cotangent[...], output_weight[...], ((1,), (1,))).astype(BF16)
    slots = jnp.where(live[...] > 0, neighbours[...], -1)
    rows = slots.shape[1]
    cap = (counts.shape[0] - rows) // 4
    entries = lax.broadcasted_iota(jnp.int32, counts.shape, 0)
    swapped = jnp.where(
        entries < rows,
        0,
        jnp.where(entries < rows + 2 * cap, 1 - places[0], 1 - places[1]),
    )
    entries = jnp.bitwise_xor(entries, swapped * cap)
    total = jnp.zeros(entries.shape, F32)
    for slot in range(slots.shape[0]):
        total = total + jnp.where(slots[slot : slot + 1, :] == entries, 1.0, 0.0)
    counts[...] = total


def attention_kernel(
    queries, key_values, grad_mixed, counts, first, cotangent, band3, band1, band2, band0,
    sent, own, back1, back2, back3, table, grads,
):
    rows, width = queries.shape
    cap = band0.shape[0]
    table[:rows, :] = key_values[...]
    for index, band in enumerate((band0, band1, band2, band3)):
        start = rows + index * cap
        table[start : start + cap, :] = band[...]
    factor = HEAD_DIM**-0.5
    count = counts[...]
    is_live = count > 0
    wide = 2 * HEAD_DIM
    side = lax.broadcasted_iota(jnp.int32, (1, wide), 1) // HEAD_DIM
    down = ((0,), (0,))
    for pair in range(HEADS // 2):
        lanes = slice(pair * wide, (pair + 1) * wide)
        value_lanes = slice(width + pair * wide, width + (pair + 1) * wide)
        query, upstream = queries[:, lanes], grad_mixed[:, lanes]
        key, value = table[:, lanes], table[:, value_lanes]
        zero = jnp.zeros((), BF16)
        mixed, grad_query, grad_key, grad_value = [], [], None, None
        for half in range(2):
            mine = side == half
            query_half = jnp.where(mine, query, zero)
            upstream_half = jnp.where(mine, upstream, zero)
            scores = dot(key, query_half, ((1,), (1,))) * factor
            grad_probs = dot(value, upstream_half, ((1,), (1,)))
            scores = jnp.where(is_live, scores, -1e30)
            row_max = jnp.max(scores, axis=0, keepdims=True)
            powers = jnp.where(is_live, jnp.exp(scores - row_max), 0.0)
            probabilities = powers / jnp.sum(count * powers, axis=0, keepdims=True)
            weights = split(count * probabilities.astype(BF16).astype(F32))
            spread = count * probabilities
            grad_scores = spread * (
                grad_probs - jnp.sum(spread * grad_probs, axis=0, keepdims=True)
            )
            grad_scores = split(grad_scores * factor)
            mixed.append(sum(dot(w, value, down) for w in weights))
            grad_query.append(sum(dot(g, key, down) for g in grad_scores))
            grad_k = sum(dot(g, query_half) for g in grad_scores)
            grad_v = sum(dot(w, upstream_half) for w in weights)
            grad_key = grad_k if half == 0 else grad_key + grad_k
            grad_value = grad_v if half == 0 else grad_value + grad_v
        sent[rows : 2 * rows, lanes] = jnp.where(side == 0, mixed[0], mixed[1]).astype(BF16)
        sent[rows : 2 * rows, value_lanes] = jnp.where(
            side == 0, grad_query[0], grad_query[1]
        ).astype(BF16)
        grads[:, lanes] = grad_key
        grads[:, value_lanes] = grad_value
    own[...] = grads[:rows, :]
    sent[2 * rows :, :] = grads[rows : rows + cap, :].astype(BF16)
    for index, back in enumerate((back1, back2, back3)):
        start = rows + (index + 1) * cap
        back[...] = grads[start : start + cap, :].astype(BF16)
    sent[:rows, :width] = first[...]
    sent[:rows, width:] = cotangent[...]


def layer_kernel(features, sent, output_weight, layer_output):
    rows, width = features.shape
    mixed = sent[rows : 2 * rows, :width]
    layer_output[...] = (features[...].astype(F32) + dot(mixed, output_weight[...])).astype(BF16)


def chosen_kernel(per_core, sent, feature_of, cell_of, partner, left, grad_output):
    width, rows = sent.shape[1] // 2, left.shape[1] // 6
    core = lax.axis_index("core")
    columns = lax.broadcasted_iota(jnp.int32, (feature_of.shape[0], width), 1)
    target = feature_of[...] + core * per_core[0]
    feature = jnp.bitwise_and(target, width - 1)
    chosen = (feature == columns).astype(F32).astype(BF16)
    part = jnp.right_shift(target, width.bit_length() - 1)
    for index, source in enumerate((sent, partner)):
        picked = dot(chosen, source[:rows, :width], ((1,), (1,)))
        for piece in range(3):
            at = (2 * piece + index) * rows
            left[:, at : at + rows] = jnp.where(part == piece, picked, 0.0).astype(BF16)
    columns = lax.broadcasted_iota(jnp.int32, (cell_of.shape[0], width), 1)
    target = cell_of[...] + core * per_core[1]
    chosen = (target == columns).astype(F32).astype(BF16)
    total = None
    for source in (sent, partner):
        picked = dot(chosen, source[:rows, width:], ((1,), (1,))).astype(BF16)
        product = dot(picked, source[rows : 2 * rows, :width])
        total = product if total is None else total + product
    grad_output[...] = total


def merge_kernel(own, send_rows, back3, back1, back2, partner, grad_keys_values):
    rows = own.shape[0]
    places = here()
    total = own[...]
    for index, back in enumerate((partner[2 * rows :, :], back1, back2, back3)):
        total = total + dot(listed(places, send_rows, index, rows), back[...])
    grad_keys_values[...] = total.astype(BF16)


def exponent(values):
    largest = jnp.max(jnp.max(jnp.abs(values), axis=0, keepdims=True), axis=1, keepdims=True)
    return jnp.floor(jnp.log2(jnp.maximum(largest, 1e-30)))


def project_kernel(left, sent, own_grads, grad_output, partner, partner_grads, both, right):
    rows, width = own_grads.shape[0], both.shape[2]
    for index, (early, late) in enumerate(((sent, own_grads), (partner, partner_grads))):
        pieces = (
            early[rows : 2 * rows, width:],
            late[:, :width],
            late[:, width:],
        )
        for piece in range(3):
            at = (2 * piece + index) * rows
            right[at : at + rows, :] = pieces[piece]
    near = both.shape[0]
    first_row = 0
    for part, values in enumerate((dot(left[...], right[...]), grad_output[...])):
        power = exponent(values)
        scaled = values * jnp.exp2(HEADROOM - power)
        count = values.shape[0] // near
        at = both.shape[1] - HEADER + part * (HEADER // 2)
        for index in range(near):
            both[index, first_row : first_row + count, :] = scaled[
                index * count : (index + 1) * count, :
            ]
            both[index, at : at + HEADER // 2, :] = jnp.broadcast_to(power, (HEADER // 2, width))
        first_row += count


def features_kernel(features, cotangent, gain, sent, late, weight, grad_features):
    rows, width = features.shape
    grad_first = dot(sent[rows : 2 * rows, width:], weight[0], ((1,), (1,)))
    for part in range(2):
        grad_first = grad_first + dot(
            late[:, part * width : (part + 1) * width], weight[1 + part], ((1,), (1,))
        )
    values = features[...].astype(F32)
    factor = norm_factor(values)
    weighted = grad_first * gain[...]
    mean = jnp.mean(values * weighted, axis=-1, keepdims=True)
    grad_features[...] = cotangent[...].astype(F32) + (
        factor * weighted - values * factor**3 * mean
    )


def near_kernel(both, summed):
    far, each = summed.shape[:2]
    width = both.shape[2]
    first_row = 0
    for part, per in enumerate((each - each // 4, each // 4)):
        at = both.shape[1] - HEADER + part * (HEADER // 2)
        total = None
        for index in range(both.shape[0]):
            scale = jnp.exp2(both[index, at : at + 1, :] - HEADROOM)
            values = both[index, first_row * far : (first_row + per) * far, :] * scale
            total = values if total is None else total + values
        power = exponent(total)
        total = total * jnp.exp2(HEADROOM - power)
        for row in range(per):
            summed[:, first_row + row, :width] = total[row * far : (row + 1) * far, :]
            summed[:, first_row + row, width:] = jnp.broadcast_to(
                power, (far, summed.shape[2] - width)
            )
        first_row += per


def far_kernel(scale, parts, grad_project, grad_output):
    lanes = grad_project.shape[1]
    per_row = (parts.shape[2] - lanes) // lanes
    width = per_row * lanes
    factors = jnp.exp2(parts[:, :, width:] - HEADROOM) * scale
    project_rows = grad_project.shape[0] // per_row
    for piece in range(per_row):
        values = parts[:, :, piece * lanes : (piece + 1) * lanes]
        total = jnp.sum(values * factors, axis=0)
        for row in range(total.shape[0]):
            if row < project_rows:
                at = row * per_row + piece
                grad_project[at : at + 1, :] = total[row : row + 1, :]
            else:
                at = (row - project_rows) * per_row + piece
                grad_output[at : at + 1, :] = total[row : row + 1, :]


def exchanged(block, axis, index):
    size = math.prod(lax.axis_size(name) for name in axis)
    partners = [i ^ 1 if index == 0 else ((i - 1) ^ 1) + 1 for i in range(size)]
    return lax.ppermute(block, axis, [(i, partner % size) for i, partner in enumerate(partners)])


def row_order(sizes, width):
    ids = np.arange(math.prod(sizes.values())).reshape([sizes[name] for name in AXES])
    ids = ids[..., 0].transpose(2, 0, 1, 3).reshape(sizes["x"], -1)
    per_project, per_output = 3 * width // (2 * ids.size), width // (2 * ids.size)

    def rows(per):
        return (ids[:, None, :] * per + np.arange(per)[None, :, None]).reshape(-1, 1)

    per_core = (per_project, per_output)
    return rows(per_project).astype(np.int32), rows(per_output).astype(np.int32), per_core


def body(features, cotangent, gain, weight, output_weight, neighbours, live, send_rows):
    rows, width = features.shape
    cap = send_rows.shape[1]
    sizes = {name: lax.axis_size(name) for name in AXES}
    devices = math.prod(sizes.values())
    scale = float(rows * devices) ** -0.5
    gain = gain.reshape(1, width)
    band = shape(cap, 2 * width)
    first, key_values, *bands = keys_call(features, gain, weight, send_rows)
    steps = ((TENSOR, 0), (TENSOR, 1), (CELLS, 0), (CELLS, 1))
    received = [exchanged(bands[index], *steps[index]) for index in (3, 1, 2, 0)]
    queries, grad_mixed, counts = call(
        queries_kernel,
        (shape(rows, width), shape(rows, width), shape(rows + 4 * cap, rows, dtype=F32)),
        (first, weight, output_weight, cotangent, neighbours.T, live.T),
        5,
    )
    sent, own, *backs = call(
        attention_kernel,
        (
            shape(2 * rows + cap, 2 * width),
            shape(rows, 2 * width, dtype=F32),
            band,
            band,
            band,
        ),
        (queries, key_values, grad_mixed, counts, first, cotangent, *received),
        8,
        moved=4,
        scratch=(
            pltpu.VMEM((rows + 4 * cap, 2 * width), BF16),
            pltpu.VMEM((rows + 4 * cap, 2 * width), F32),
        ),
    )
    returned = [exchanged(backs[index - 1], *steps[index]) for index in (3, 1, 2)]
    partner = exchanged(sent, *steps[0])
    layer_output = call(
        layer_kernel, shape(rows, width), (features, sent, output_weight), 3
    )
    feature_of, cell_of, per_core = row_order(sizes, width)
    near = sizes["x"]
    far = devices // (2 * near)
    left, grad_output = call(
        functools.partial(chosen_kernel, per_core),
        (shape(3 * width // 2, 6 * rows), shape(width // 2, width, dtype=F32)),
        (sent, feature_of, cell_of, partner),
        3,
        moved=1,
    )
    grad_keys_values = call(
        merge_kernel,
        shape(rows, 2 * width),
        (own, send_rows, *returned, partner),
        2,
        moved=4,
    )
    partner_grads = exchanged(grad_keys_values, *steps[0])
    both = call(
        project_kernel,
        shape(near, 2 * width // near + HEADER, width, dtype=F32),
        (left, sent, grad_keys_values, grad_output, partner, partner_grads),
        3,
        moved=2,
        scratch=(pltpu.VMEM((6 * rows, width), BF16),),
    )
    both = lax.all_to_all(both.astype(jnp.float16), "x", 0, 0, tiled=True).astype(F32)
    grad_features = call(
        features_kernel,
        shape(rows, width, dtype=F32),
        (features, cotangent, gain, sent, grad_keys_values, weight),
        3,
    )
    parts = call(
        near_kernel, shape(far, 4 * width // devices, width + 128, dtype=F32), (both,), 2, moved=1
    )
    parts = lax.all_to_all(parts.astype(jnp.float16), FAR, 0, 0, tiled=True).astype(F32)
    grad_project, grad_output = call(
        functools.partial(far_kernel, scale),
        tuple(shape(count * width * width // devices // 128, 128, dtype=F32) for count in (3, 1)),
        (parts,),
        2,
        moved=1,
    )
    return layer_output, grad_features, grad_project.reshape(-1), grad_output.reshape(-1)


def split_mesh(mesh):
    if mesh.devices.size == 512:
        sizes = (2, 8, 4, 4, 2)
    else:
        sizes = (1, 2, mesh.devices.shape[0] // 2, mesh.devices.shape[1] // 2, 2)
    return Mesh(mesh.devices.reshape(sizes), AXES)


def solution(mesh):
    mesh = split_mesh(mesh)
    by_cell = P(AXES, None)
    return jax.shard_map(
        body,
        mesh=mesh,
        in_specs=(by_cell, by_cell, P(), P(), P(), by_cell, by_cell, by_cell),
        out_specs=(by_cell, by_cell, P(AXES), P(AXES)),
        check_vma=False,
    )
```

```python
import functools
import math

import jax
import jax.numpy as jnp
import numpy as np
from jax import lax
from jax.experimental import pallas as pl
from jax.experimental.pallas import tpu as pltpu
from jax.sharding import Mesh
from jax.sharding import PartitionSpec as P


HEADS = 8
HEAD_DIM = 64
EPSILON = 1e-06
HEADER = 16
HEADROOM = 13.0
VMEM_BYTES = 16 * 1024 * 1024
F32 = jnp.float32
BF16 = jnp.bfloat16
AXES = ("yh", "z", "x", "yl", "core")
CELLS = ("yh", "z", "x")
TENSOR = ("yl", "core")
FAR = ("yh", "z", "yl")


def dot(a, b, dims=((1,), (0,))):
    return lax.dot_general(a, b, (dims, ((), ())), preferred_element_type=F32)


def split(values):
    high = values.astype(BF16)
    return high, (values - high.astype(F32)).astype(BF16)


def call(kernel, out_shapes, args, us, moved=0, scratch=()):
    held = len(args) - moved
    specs = [pl.BlockSpec(memory_space=pltpu.VMEM)] * held
    specs += [pl.BlockSpec(memory_space=pl.ANY)] * moved
    scratch = list(scratch)
    if moved:
        scratch += [pltpu.VMEM(arg.shape, arg.dtype) for arg in args[held:]]
        scratch.append(pltpu.SemaphoreType.DMA((moved,)))

    def moving(*refs):
        away, local, arrived = refs[held : len(args)], refs[-1 - moved : -1], refs[-1]
        copies = [
            pltpu.make_async_copy(away[index], local[index], arrived.at[index])
            for index in range(moved)
        ]
        for copy in copies:
            copy.start()
        for copy in copies:
            copy.wait()
        kernel(*refs[:held], *local, *refs[len(args) : -1 - moved])

    return pl.pallas_call(
        moving if moved else kernel,
        out_shape=out_shapes,
        in_specs=specs,
        out_specs=jax.tree.map(lambda _: pl.BlockSpec(memory_space=pltpu.VMEM), out_shapes),
        scratch_shapes=scratch,
        compiler_params=pltpu.CompilerParams(vmem_limit_bytes=VMEM_BYTES),
        cost_estimate=pl.CostEstimate(
            flops=int(us * 4e8), bytes_accessed=int(us * 1e6), transcendentals=0
        ),
    )(*args)


def shape(*dims, dtype=BF16):
    return jax.ShapeDtypeStruct(dims, dtype)


def norm_factor(values):
    return lax.rsqrt(jnp.mean(values * values, axis=-1, keepdims=True) + EPSILON)


def here():
    return lax.axis_index("core"), lax.rem(lax.axis_index("x"), 2)


def listed(places, send_rows, index, rows):
    first = 2 * (index // 2)
    at_even, at_odd = first + index % 2, first + 1 - index % 2
    chosen = jnp.where(
        places[index // 2] == 0,
        send_rows[at_even : at_even + 1, :],
        send_rows[at_odd : at_odd + 1, :],
    )
    row_ids = lax.broadcasted_iota(jnp.int32, (rows, send_rows.shape[1]), 0)
    return (row_ids == chosen).astype(F32).astype(BF16)


def keys_kernel(
    features_hbm, gain_hbm, weight_hbm, send_rows_hbm,
    first, key_values, band0, band1, band2, band3,
    features, gain, weight, send_rows, arrived,
):
    copies = [
        pltpu.make_async_copy(source, local, arrived.at[index])
        for index, (source, local) in enumerate(
            (
                (features_hbm, features),
                (gain_hbm, gain),
                (weight_hbm.at[1], weight.at[0]),
                (weight_hbm.at[2], weight.at[1]),
                (send_rows_hbm, send_rows),
            )
        )
    ]
    for copy in copies:
        copy.start()
    copies[0].wait()
    copies[1].wait()
    values = features[...].astype(F32)
    normed = (values * norm_factor(values) * gain[...]).astype(BF16)
    first[...] = normed
    width = weight.shape[2]
    for part in range(2):
        copies[2 + part].wait()
        key_values[:, part * width : (part + 1) * width] = dot(normed, weight[part]).astype(BF16)
    copies[4].wait()
    table = key_values[...]
    places = here()
    for index, band in enumerate((band0, band1, band2, band3)):
        chosen = listed(places, send_rows, index, features.shape[0])
        band[...] = dot(chosen, table, ((0,), (0,))).astype(BF16)


def keys_call(features, gain, weight, send_rows):
    rows, width = features.shape
    band = shape(send_rows.shape[1], 2 * width)
    vmem = pl.BlockSpec(memory_space=pltpu.VMEM)
    return pl.pallas_call(
        keys_kernel,
        out_shape=(shape(rows, width), shape(rows, 2 * width), band, band, band, band),
        in_specs=[pl.BlockSpec(memory_space=pltpu.HBM)] * 4,
        out_specs=(vmem,) * 6,
        scratch_shapes=[
            pltpu.VMEM(features.shape, BF16),
            pltpu.VMEM(gain.shape, F32),
            pltpu.VMEM((2, width, width), BF16),
            pltpu.VMEM(send_rows.shape, jnp.int32),
            pltpu.SemaphoreType.DMA((5,)),
        ],
        compiler_params=pltpu.CompilerParams(vmem_limit_bytes=VMEM_BYTES),
        cost_estimate=pl.CostEstimate(
            flops=1200000000, bytes_accessed=3000000, transcendentals=0
        ),
    )(
        *(
            pltpu.with_memory_space_constraint(array, pltpu.HBM)
            for array in (features, gain, weight, send_rows)
        )
    )


def queries_kernel(
    first, weight, output_weight, cotangent, neighbours, live, queries, grad_mixed, counts
):
    places = here()
    queries[...] = dot(first[...], weight[0]).astype(BF16)
    grad_mixed[...] = dot(cotangent[...], output_weight[...], ((1,), (1,))).astype(BF16)
    slots = jnp.where(live[...] > 0, neighbours[...], -1)
    rows = slots.shape[1]
    cap = (counts.shape[0] - rows) // 4
    entries = lax.broadcasted_iota(jnp.int32, counts.shape, 0)
    swapped = jnp.where(
        entries < rows,
        0,
        jnp.where(entries < rows + 2 * cap, 1 - places[0], 1 - places[1]),
    )
    entries = jnp.bitwise_xor(entries, swapped * cap)
    total = jnp.zeros(entries.shape, F32)
    for slot in range(slots.shape[0]):
        total = total + jnp.where(slots[slot : slot + 1, :] == entries, 1.0, 0.0)
    counts[...] = total


def attention_kernel(
    queries, key_values, grad_mixed, counts, first, cotangent, band3, band1, band2, band0,
    sent, own, back1, back2, back3, table, grads,
):
    rows, width = queries.shape
    cap = band0.shape[0]
    table[:rows, :] = key_values[...]
    for index, band in enumerate((band0, band1, band2, band3)):
        start = rows + index * cap
        table[start : start + cap, :] = band[...]
    factor = HEAD_DIM**-0.5
    count = jnp.concatenate([counts[...], counts[...]], axis=1)
    is_live = count > 0
    wide = 2 * HEAD_DIM
    side = lax.broadcasted_iota(jnp.int32, (1, wide), 1) // HEAD_DIM
    down = ((0,), (0,))
    zero = jnp.zeros((), BF16)

    def halves(block):
        return jnp.concatenate([jnp.where(side == half, block, zero) for half in range(2)], axis=0)

    def joined(block):
        return jnp.where(side == 0, block[:rows, :], block[rows:, :]).astype(BF16)

    for pair in range(HEADS // 2):
        lanes = slice(pair * wide, (pair + 1) * wide)
        value_lanes = slice(width + pair * wide, width + (pair + 1) * wide)
        query, upstream = halves(queries[:, lanes]), halves(grad_mixed[:, lanes])
        key, value = table[:, lanes], table[:, value_lanes]
        scores = dot(key, query, ((1,), (1,))) * factor
        grad_probs = dot(value, upstream, ((1,), (1,)))
        scores = jnp.where(is_live, scores, -1e30)
        row_max = jnp.max(scores, axis=0, keepdims=True)
        powers = jnp.where(is_live, jnp.exp(scores - row_max), 0.0)
        probabilities = powers / jnp.sum(count * powers, axis=0, keepdims=True)
        weights = split(count * probabilities.astype(BF16).astype(F32))
        spread = count * probabilities
        grad_scores = spread * (
            grad_probs - jnp.sum(spread * grad_probs, axis=0, keepdims=True)
        )
        grad_scores = split(grad_scores * factor)
        sent[rows : 2 * rows, lanes] = joined(sum(dot(w, value, down) for w in weights))
        sent[rows : 2 * rows, value_lanes] = joined(sum(dot(g, key, down) for g in grad_scores))
        grads[:, lanes] = sum(dot(g, query) for g in grad_scores)
        grads[:, value_lanes] = sum(dot(w, upstream) for w in weights)
    own[...] = grads[:rows, :]
    sent[2 * rows :, :] = grads[rows : rows + cap, :].astype(BF16)
    for index, back in enumerate((back1, back2, back3)):
        start = rows + (index + 1) * cap
        back[...] = grads[start : start + cap, :].astype(BF16)
    sent[:rows, :width] = first[...]
    sent[:rows, width:] = cotangent[...]


def layer_kernel(features, sent, output_weight, layer_output):
    rows, width = features.shape
    mixed = sent[rows : 2 * rows, :width]
    layer_output[...] = (features[...].astype(F32) + dot(mixed, output_weight[...])).astype(BF16)


def chosen_kernel(per_core, sent, feature_of, cell_of, partner, left, grad_output):
    width, rows = sent.shape[1] // 2, left.shape[1] // 6
    core = lax.axis_index("core")
    columns = lax.broadcasted_iota(jnp.int32, (feature_of.shape[0], width), 1)
    target = feature_of[...] + core * per_core[0]
    feature = jnp.bitwise_and(target, width - 1)
    chosen = (feature == columns).astype(F32).astype(BF16)
    part = jnp.right_shift(target, width.bit_length() - 1)
    for index, source in enumerate((sent, partner)):
        picked = dot(chosen, source[:rows, :width], ((1,), (1,)))
        for piece in range(3):
            at = (2 * piece + index) * rows
            left[:, at : at + rows] = jnp.where(part == piece, picked, 0.0).astype(BF16)
    columns = lax.broadcasted_iota(jnp.int32, (cell_of.shape[0], width), 1)
    target = cell_of[...] + core * per_core[1]
    chosen = (target == columns).astype(F32).astype(BF16)
    total = None
    for source in (sent, partner):
        picked = dot(chosen, source[:rows, width:], ((1,), (1,))).astype(BF16)
        product = dot(picked, source[rows : 2 * rows, :width])
        total = product if total is None else total + product
    grad_output[...] = total


def merge_kernel(own, send_rows, back3, back1, back2, partner, grad_keys_values):
    rows = own.shape[0]
    places = here()
    total = own[...]
    for index, back in enumerate((partner[2 * rows :, :], back1, back2, back3)):
        total = total + dot(listed(places, send_rows, index, rows), back[...])
    grad_keys_values[...] = total.astype(BF16)


def exponent(values):
    largest = jnp.max(jnp.max(jnp.abs(values), axis=0, keepdims=True), axis=1, keepdims=True)
    return jnp.floor(jnp.log2(jnp.maximum(largest, 1e-30)))


def project_kernel(left, sent, own_grads, grad_output, partner, partner_grads, both, right):
    rows, width = own_grads.shape[0], both.shape[2]
    for index, (early, late) in enumerate(((sent, own_grads), (partner, partner_grads))):
        pieces = (
            early[rows : 2 * rows, width:],
            late[:, :width],
            late[:, width:],
        )
        for piece in range(3):
            at = (2 * piece + index) * rows
            right[at : at + rows, :] = pieces[piece]
    near = both.shape[0]
    first_row = 0
    for part, values in enumerate((dot(left[...], right[...]), grad_output[...])):
        power = exponent(values)
        scaled = values * jnp.exp2(HEADROOM - power)
        count = values.shape[0] // near
        at = both.shape[1] - HEADER + part * (HEADER // 2)
        for index in range(near):
            both[index, first_row : first_row + count, :] = scaled[
                index * count : (index + 1) * count, :
            ]
            both[index, at : at + HEADER // 2, :] = jnp.broadcast_to(power, (HEADER // 2, width))
        first_row += count


def features_kernel(features, cotangent, gain, sent, late, weight, grad_features):
    rows, width = features.shape
    grad_first = dot(sent[rows : 2 * rows, width:], weight[0], ((1,), (1,)))
    for part in range(2):
        grad_first = grad_first + dot(
            late[:, part * width : (part + 1) * width], weight[1 + part], ((1,), (1,))
        )
    values = features[...].astype(F32)
    factor = norm_factor(values)
    weighted = grad_first * gain[...]
    mean = jnp.mean(values * weighted, axis=-1, keepdims=True)
    grad_features[...] = cotangent[...].astype(F32) + (
        factor * weighted - values * factor**3 * mean
    )


def near_kernel(both, summed):
    far, each = summed.shape[:2]
    width = both.shape[2]
    first_row = 0
    for part, per in enumerate((each - each // 4, each // 4)):
        at = both.shape[1] - HEADER + part * (HEADER // 2)
        total = None
        for index in range(both.shape[0]):
            scale = jnp.exp2(both[index, at : at + 1, :] - HEADROOM)
            values = both[index, first_row * far : (first_row + per) * far, :] * scale
            total = values if total is None else total + values
        power = exponent(total)
        total = total * jnp.exp2(HEADROOM - power)
        for row in range(per):
            summed[:, first_row + row, :width] = total[row * far : (row + 1) * far, :]
            summed[:, first_row + row, width:] = jnp.broadcast_to(
                power, (far, summed.shape[2] - width)
            )
        first_row += per


def far_kernel(scale, parts, grad_project, grad_output):
    lanes = grad_project.shape[1]
    per_row = (parts.shape[2] - lanes) // lanes
    width = per_row * lanes
    factors = jnp.exp2(parts[:, :, width:] - HEADROOM) * scale
    project_rows = grad_project.shape[0] // per_row
    for piece in range(per_row):
        values = parts[:, :, piece * lanes : (piece + 1) * lanes]
        total = jnp.sum(values * factors, axis=0)
        for row in range(total.shape[0]):
            if row < project_rows:
                at = row * per_row + piece
                grad_project[at : at + 1, :] = total[row : row + 1, :]
            else:
                at = (row - project_rows) * per_row + piece
                grad_output[at : at + 1, :] = total[row : row + 1, :]


def exchanged(block, axis, index):
    size = math.prod(lax.axis_size(name) for name in axis)
    partners = [i ^ 1 if index == 0 else ((i - 1) ^ 1) + 1 for i in range(size)]
    return lax.ppermute(block, axis, [(i, partner % size) for i, partner in enumerate(partners)])


def row_order(sizes, width):
    ids = np.arange(math.prod(sizes.values())).reshape([sizes[name] for name in AXES])
    ids = ids[..., 0].transpose(2, 0, 1, 3).reshape(sizes["x"], -1)
    per_project, per_output = 3 * width // (2 * ids.size), width // (2 * ids.size)

    def rows(per):
        return (ids[:, None, :] * per + np.arange(per)[None, :, None]).reshape(-1, 1)

    per_core = (per_project, per_output)
    return rows(per_project).astype(np.int32), rows(per_output).astype(np.int32), per_core


def body(features, cotangent, gain, weight, output_weight, neighbours, live, send_rows):
    rows, width = features.shape
    cap = send_rows.shape[1]
    sizes = {name: lax.axis_size(name) for name in AXES}
    devices = math.prod(sizes.values())
    scale = float(rows * devices) ** -0.5
    gain = gain.reshape(1, width)
    band = shape(cap, 2 * width)
    first, key_values, *bands = keys_call(features, gain, weight, send_rows)
    steps = ((TENSOR, 0), (TENSOR, 1), (CELLS, 0), (CELLS, 1))
    received = [exchanged(bands[index], *steps[index]) for index in (3, 1, 2, 0)]
    queries, grad_mixed, counts = call(
        queries_kernel,
        (shape(rows, width), shape(rows, width), shape(rows + 4 * cap, rows, dtype=F32)),
        (first, weight, output_weight, cotangent, neighbours.T, live.T),
        5,
    )
    sent, own, *backs = call(
        attention_kernel,
        (
            shape(2 * rows + cap, 2 * width),
            shape(rows, 2 * width, dtype=F32),
            band,
            band,
            band,
        ),
        (queries, key_values, grad_mixed, counts, first, cotangent, *received),
        8,
        moved=4,
        scratch=(
            pltpu.VMEM((rows + 4 * cap, 2 * width), BF16),
            pltpu.VMEM((rows + 4 * cap, 2 * width), F32),
        ),
    )
    returned = []
    for index in (3, 1, 2):
        returned.append(exchanged(backs[index - 1], *steps[index]))
    partner = exchanged(sent, *steps[0])
    layer_output = call(
        layer_kernel, shape(rows, width), (features, sent, output_weight), 3
    )
    feature_of, cell_of, per_core = row_order(sizes, width)
    near = sizes["x"]
    far = devices // (2 * near)
    left, grad_output = call(
        functools.partial(chosen_kernel, per_core),
        (shape(3 * width // 2, 6 * rows), shape(width // 2, width, dtype=F32)),
        (sent, feature_of, cell_of, partner),
        3,
        moved=1,
    )
    grad_keys_values = call(
        merge_kernel,
        shape(rows, 2 * width),
        (own, send_rows, *returned, partner),
        2,
        moved=4,
    )
    partner_grads = exchanged(grad_keys_values, *steps[0])
    both = call(
        project_kernel,
        shape(near, 2 * width // near + HEADER, width, dtype=F32),
        (left, sent, grad_keys_values, grad_output, partner, partner_grads),
        3,
        moved=2,
        scratch=(pltpu.VMEM((6 * rows, width), BF16),),
    )
    both = lax.all_to_all(both.astype(jnp.float16), "x", 0, 0, tiled=True).astype(F32)
    grad_features = call(
        features_kernel,
        shape(rows, width, dtype=F32),
        (features, cotangent, gain, sent, grad_keys_values, weight),
        3,
    )
    parts = call(
        near_kernel, shape(far, 4 * width // devices, width + 128, dtype=F32), (both,), 2, moved=1
    )
    parts = lax.all_to_all(parts.astype(jnp.float16), FAR, 0, 0, tiled=True).astype(F32)
    grad_project, grad_output = call(
        functools.partial(far_kernel, scale),
        tuple(shape(count * width * width // devices // 128, 128, dtype=F32) for count in (3, 1)),
        (parts,),
        2,
        moved=1,
    )
    return layer_output, grad_features, grad_project.reshape(-1), grad_output.reshape(-1)


def split_mesh(mesh):
    if mesh.devices.size == 512:
        sizes = (2, 8, 4, 4, 2)
    else:
        sizes = (1, 2, mesh.devices.shape[0] // 2, mesh.devices.shape[1] // 2, 2)
    return Mesh(mesh.devices.reshape(sizes), AXES)


def solution(mesh):
    mesh = split_mesh(mesh)
    by_cell = P(AXES, None)
    return jax.shard_map(
        body,
        mesh=mesh,
        in_specs=(by_cell, by_cell, P(), P(), P(), by_cell, by_cell, by_cell),
        out_specs=(by_cell, by_cell, P(AXES), P(AXES)),
        check_vma=False,
    )
```
